256 devices in a mesh: tracer: 8 (over y, x_lo), gx: 4 (over x_hi, core), gy: 8 (over z).
Axes of the slice: x: 4 (x_hi: 2, x_lo: 2; x = x_hi * 2 + x_lo), y: 4, z: 8, core: 2. Of those that a mesh axis runs over, the one named last changes fastest.
Arguments:
- tracers: float32 [96, 16, 32, 1024], P('tracer', None, 'gx', 'gy'), may hold values from 0.05 to 2
- fluxes: float32 [3, 16, 32, 1024], P(None, 'tracer', 'gx', 'gy'), may hold values from -0.15 to 0.15
- diff_east: float32 [32, 1024], P('gx', 'gy'), may hold values from 0.01 to 0.1
- diff_north: float32 [32, 1024], P('gx', 'gy'), may hold values from 0.01 to 0.1
- column_depth: int32 [32, 1024], P('gx', 'gy'), may hold values from 0 to 16
- grazers: float32 [16, 32, 1024], P(None, 'gx', 'gy'), may hold values from 0.2 to 0.9
- groups: int32 [96], P('tracer'), may hold values from 0 to 15
- preference: float32 [16], replicated, may hold values from 0.1 to 1
Outputs:
- advanced: float32 [96, 16, 32, 1024], P('tracer', None, 'gx', 'gy')
The draws below stay inside these ranges and needn't reach their ends.
Inputs may be any that keep to these rules, and one draw needn't show every extreme that they name: A cell at level k is sea iff k < column_depth of its column.
All inputs are finite; a program needn't handle non-finite values.
Results may differ from the reference program's by a relative error of at most 0.0003.
Values sent between devices are 32-bit elements; how exact they have to be, the bound alone decides.
A program may use at most 64 MiB of HBM per device.

```python
import math
import jax
import jax.numpy as jnp
from jax import lax

GROUPS = 16
LEV = 16
STEPS = 2
TRACERS = 96
NX = 32
NY = 1024


def place_ends(result, stream_key, low, top_value):
    shape = result.shape
    place = [jax.random.randint(jax.random.fold_in(stream_key, axis), (), 0, shape[axis]) for axis in range(len(shape))]
    result = result.at[tuple(place)].set(low)
    longest = shape.index(max(shape))
    place[longest] = (place[longest] + 1) % shape[longest]
    return result.at[tuple(place)].set(top_value)


def block_scale(own_key, shape, shards, low, largest):
    factor_of = 1.0
    for axis_at, shards_of in shards:
        steps = jax.random.uniform(jax.random.fold_in(jax.random.fold_in(own_key, 6), axis_at), (shards_of,), jnp.float32, low / len(shards), largest / len(shards))
        factor_of = factor_of * jnp.repeat(jnp.exp(steps), shape[axis_at] // shards_of).reshape((-1,) + (1,) * (len(shape) - 1 - axis_at))
    return factor_of


def setup_inputs(seed: int = 0) -> dict:
    splits = jax.random.split(jax.random.key(seed), 9)
    return {
        "tracers": jnp.clip(jnp.exp(math.log(2.0) - 3.6888794 * jax.random.uniform(splits[0], (TRACERS, LEV, NX, NY), jnp.float32) ** block_scale(splits[0], (TRACERS, LEV, NX, NY), ((0, 8), (2, 4), (3, 8)), -0.2, 0.2)), 0.05, 2.0),
        "fluxes": jnp.clip(jax.random.uniform(splits[1], (3, LEV, NX, NY), jnp.float32, -0.15, 0.15) * block_scale(splits[1], (3, LEV, NX, NY), ((1, 8), (2, 4), (3, 8)), -0.4, 0.0), -0.15, 0.15),
        "diff_east": jnp.clip(jnp.exp(math.log(0.1) - 2.3025851 * jax.random.uniform(splits[2], (NX, NY), jnp.float32) ** block_scale(splits[2], (NX, NY), ((0, 4), (1, 8)), -0.2, 0.2)), 0.01, 0.1),
        "diff_north": jnp.clip(jnp.exp(math.log(0.1) - 2.3025851 * jax.random.uniform(splits[3], (NX, NY), jnp.float32) ** block_scale(splits[3], (NX, NY), ((0, 4), (1, 8)), -0.2, 0.2)), 0.01, 0.1),
        "column_depth": place_ends(jax.random.randint(splits[4], (NX, NY), 0, LEV + 1), jax.random.fold_in(splits[4], 1), 0, LEV).astype(jnp.int32),
        "grazers": jnp.clip(jnp.exp(math.log(0.9) - 1.50407736 * jax.random.uniform(splits[5], (LEV, NX, NY), jnp.float32) ** block_scale(splits[5], (LEV, NX, NY), ((1, 4), (2, 8)), -0.2, 0.2)), 0.2, 0.9),
        "groups": place_ends(jax.random.randint(splits[6], (TRACERS,), 0, GROUPS), jax.random.fold_in(splits[6], 1), 0, GROUPS - 1).astype(jnp.int32),
        "preference": jnp.clip(jnp.exp(jax.random.uniform(splits[7], (GROUPS,), jnp.float32, math.log(0.1), math.log(1.0))), 0.1, 1.0),
    }


def minmod(jump_low, jump_high):
    return jnp.maximum(0.0, jnp.minimum(jump_low, jump_high)) + jnp.minimum(0.0, jnp.maximum(jump_low, jump_high))


def window(values, low_end, high_end, direction):
    return lax.slice_in_dim(values, low_end, high_end, axis=direction % values.ndim)


def face_terms(tracer_field, open_faces, face_flux, face_kappa, direction):
    length = tracer_field.shape[direction % tracer_field.ndim] - 4
    jump_face = open_faces * (window(tracer_field, 1, length + 4, direction) - window(tracer_field, 0, length + 3, direction))
    slopes = minmod(window(jump_face, 0, length + 2, direction), window(jump_face, 1, length + 3, direction))
    left_value = window(tracer_field, 1, length + 2, direction) + 0.5 * window(slopes, 0, length + 1, direction)
    right_value = window(tracer_field, 2, length + 3, direction) - 0.5 * window(slopes, 1, length + 2, direction)
    carried = face_flux * jnp.where(face_flux > 0.0, left_value, right_value)
    if face_kappa is not None:
        carried = carried - face_kappa * window(jump_face, 1, length + 2, direction)
    return window(carried, 0, length, direction) - window(carried, 1, length + 1, direction)


def reference(tracers, fluxes, diff_east, diff_north, column_depth, grazers, groups, preference):
    level_index = lax.broadcasted_iota(jnp.int32, (LEV, NX, NY), 0)
    wet_cells = (level_index < column_depth[None]).astype(jnp.float32)
    wet_padded = jnp.pad(wet_cells, 2)
    open_x = wet_padded[2:-2, :-1, 2:-2] * wet_padded[2:-2, 1:, 2:-2]
    open_y = wet_padded[2:-2, 2:-2, :-1] * wet_padded[2:-2, 2:-2, 1:]
    open_z = wet_padded[:-1, 2:-2, 2:-2] * wet_padded[1:, 2:-2, 2:-2]
    flux_x = jnp.pad(fluxes[0], ((0, 0), (1, 0), (0, 0))) * open_x[:, 1:NX + 2]
    kappa_x = jnp.pad(diff_east, ((1, 0), (0, 0)))[None] * open_x[:, 1:NX + 2]
    flux_y = jnp.pad(fluxes[1], ((0, 0), (0, 0), (1, 0))) * open_y[:, :, 1:NY + 2]
    kappa_y = jnp.pad(diff_north, ((0, 0), (1, 0)))[None] * open_y[:, :, 1:NY + 2]
    flux_z = jnp.pad(fluxes[2], ((1, 0), (0, 0), (0, 0))) * open_z[1:LEV + 2]
    group_match = (groups[:, None] == lax.broadcasted_iota(jnp.int32, (1, GROUPS), 1)).astype(jnp.float32)
    grazing_pref = jnp.sum(group_match * preference[None, :], axis=1)
    tracer_field = tracers
    for step_index in range(STEPS):
        prey_total = jnp.einsum("t,tlxy->lxy", grazing_pref, tracer_field)
        factor = grazers / (1.0 + 4.0 * prey_total / TRACERS)

        def advance_tracer(items):
            single, pref_one = items
            tendency = face_terms(jnp.pad(single, ((0, 0), (2, 2), (0, 0))), open_x, flux_x, kappa_x, -2)
            tendency = tendency + face_terms(jnp.pad(single, ((0, 0), (0, 0), (2, 2))), open_y, flux_y, kappa_y, -1)
            tendency = tendency + face_terms(jnp.pad(single, ((2, 2), (0, 0), (0, 0))), open_z, flux_z, None, -3)
            return single + tendency - (pref_one * factor) * single

        tracer_field = lax.map(advance_tracer, (tracer_field, grazing_pref))
    return tracer_field
```

```python
import functools

import jax
import jax.numpy as jnp
from jax import lax
from jax.experimental import pallas as pl
from jax.experimental.pallas import tpu as pltpu
from jax.sharding import PartitionSpec as P

STEPS = 2
MESH = pl.DeviceIdType.MESH
F32 = jnp.float32
LANES = 128
LO, IN, HI = 6, 8, 16


def minmod(a, b):
    return jnp.maximum(0.0, jnp.minimum(a, b)) + jnp.minimum(0.0, jnp.maximum(a, b))


def roll(v, shift):
    return pltpu.roll(v, shift % LANES, 1)


def kernel(
    dims, tr, fl, de, dn, dep, gz, grp, prf, out,
    ext, adv, outv, flv, dev, dnv, depv, gzv, grps, prfs, tv,
    cxs, cxl, cxh, cys, cyl, cyh, fa, fb, fx,
    pqs, pqr, rs, rr, f1, f2, own1,
    sxl, sxh, xl, xh, yp, yl, yr, g1, g2,
    hy, fy, ky, hz, fz, hx, kx, wx, ec,
    lsem, csem, crec, fas, far, fbs, fbr, pqss, pqrs, rss, rrs, f1s, f1r, f2s, f2r,
    xss, xrs, yss, yrs, osem,
):
    nt, nx, ny, t_dev, lev, total = dims
    own = lev // nt
    me, gx, gy = lax.axis_index("tracer"), lax.axis_index("gx"), lax.axis_index("gy")
    left, right = lax.rem(gy + ny - 1, ny), lax.rem(gy + 1, ny)
    has_lo, has_hi = gx > 0, gx < nx - 1
    others = [lax.rem(me + d, nt) for d in range(1, nt)]

    loads = [
        (tr, ext.at[0, :, :, pl.ds(IN, 8), :]), (fl, flv), (de, dev), (dn, dnv), (dep, depv),
        (gz, gzv), (grp, grps), (prf, prfs),
    ]
    loads = [pltpu.make_async_copy(a, b, lsem.at[i]) for i, (a, b) in enumerate(loads)]

    barrier = pltpu.get_barrier_semaphore()
    for peer in others:
        pl.semaphore_signal(barrier, inc=1, device_id={"tracer": peer}, device_id_type=MESH)
    for z in (left, right):
        pl.semaphore_signal(barrier, inc=1, device_id={"gy": z}, device_id_type=MESH)

    @pl.when(has_lo)
    def _():
        pl.semaphore_signal(barrier, inc=1, device_id={"gx": gx - 1}, device_id_type=MESH)

    @pl.when(has_hi)
    def _():
        pl.semaphore_signal(barrier, inc=1, device_id={"gx": gx + 1}, device_id_type=MESH)

    for c in loads:
        c.start()

    lane = lax.broadcasted_iota(jnp.int32, (8, LANES), 1)
    row = lax.broadcasted_iota(jnp.int32, (8, LANES), 0)
    quad, e = lane // 4, lane % 4
    plev = quad % lev
    lane0, lane127 = lane == 0, lane == LANES - 1
    zero = jnp.zeros((8, LANES), F32)

    def spread(v):
        base = jnp.where(lane < 4, roll(v, 2), zero)
        for s in (4, 8, 16, 32, 64):
            base = base + roll(base, s)
        return base

    for c in loads[1:]:
        c.wait()
    for t in range(t_dev):
        tv[t] = jnp.full((8, LANES), prfs[grps[t]], F32)
    depth = depv[...].astype(F32)
    cxs[0] = depth
    cxs[1] = dev[...]
    rows_tile = zero
    lanes_tile = zero
    for b in range(own):
        rows_tile = jnp.where(row == b, flv[0, b, pl.ds(7, 1), :], rows_tile)
        col = spread(flv[1, b])
        lanes_tile = jnp.where((plev == me * own + b) & (e == 2), roll(col, 1), lanes_tile)
    cxs[2] = rows_tile
    cys[0] = spread(depth)
    cys[1] = spread(dnv[...])
    cys[2] = lanes_tile
    for k in range(3):
        for b in range(own):
            fa[me, k * own + b] = flv[k, b]
    fa[me, 3 * own] = lanes_tile
    loads[0].wait()

    def send(src, dst, ssem, rsem, to):
        return pltpu.make_async_remote_copy(
            src_ref=src, dst_ref=dst, send_sem=ssem, recv_sem=rsem, device_id=to, device_id_type=MESH
        )

    def pack_level(s, l, tiles, acc):
        acc = list(acc)
        for t in range(t_dev):
            sxl[s, l, pl.ds(2 * t, 2), :] = ext[s, t, l, pl.ds(IN, 2), :]
            sxh[s, l, pl.ds(2 * t, 2), :] = ext[s, t, l, pl.ds(IN + 6, 2), :]
            q = (t % 2) * lev + l
            acc[t // 2] = jnp.where(quad == q, pltpu.roll(tiles[t], lax.rem(4 * q + 2, LANES), 1), acc[t // 2])
        return tuple(acc)

    def first(l, acc):
        tiles = [ext[0, t, l, pl.ds(IN, 8), :] for t in range(t_dev)]
        p_sum, q_sum = zero, zero
        for t in range(t_dev):
            w = tv[t]
            wc = w * tiles[t]
            p_sum = p_sum + wc
            q_sum = q_sum + w * wc
        j, b = l // own, lax.rem(l, own)
        pqs[j, b] = p_sum
        pqs[j, own + b] = q_sum
        return pack_level(0, l, tiles, acc)

    acc = lax.fori_loop(0, lev, first, tuple(zero for _ in range(t_dev // 2)))
    for p in range(t_dev // 2):
        yp[0, p] = acc[p]

    pl.semaphore_wait(barrier, nt - 1 + 2 + has_lo.astype(jnp.int32) + has_hi.astype(jnp.int32))

    c_right = send(cys, cyl, csem.at[0], crec.at[0], {"gy": right})
    c_left = send(cys.at[pl.ds(0, 1)], cyh, csem.at[1], crec.at[1], {"gy": left})
    c_up = send(cxs, cxl, csem.at[2], crec.at[2], {"gx": gx + 1})
    c_down = send(cxs.at[pl.ds(0, 1)], cxh, csem.at[3], crec.at[3], {"gx": gx - 1})
    c_right.start()
    c_left.start()
    pl.when(has_hi)(c_up.start)
    pl.when(has_lo)(c_down.start)

    def y_copies(s):
        return (
            send(yp.at[s], yl.at[s], yss.at[s, 0], yrs.at[s, 0], {"gy": right}),
            send(yp.at[s], yr.at[s], yss.at[s, 1], yrs.at[s, 1], {"gy": left}),
        )

    def x_copies(s, j):
        c = pl.ds(j * own, own)
        return (
            send(sxh.at[s, c], xl.at[s, c], xss.at[s, 0, j], xrs.at[s, 0, j], {"gx": gx + 1}),
            send(sxl.at[s, c], xh.at[s, c], xss.at[s, 1, j], xrs.at[s, 1, j], {"gx": gx - 1}),
        )

    def gather_start(buf, ssem, rsem):
        for d, peer in enumerate(others):
            send(buf.at[me], buf.at[me], ssem.at[d], rsem.at[me], {"tracer": peer}).start()

    def gather_wait(buf, ssem, rsem):
        for d, peer in enumerate(others):
            send(buf.at[me], buf.at[peer], ssem.at[d], rsem.at[peer], {"tracer": peer}).wait_recv()

    def gather_done(buf, ssem, rsem):
        for d, peer in enumerate(others):
            send(buf.at[me], buf.at[peer], ssem.at[d], rsem.at[peer], {"tracer": peer}).wait_send()

    def scatter(src, dst, ssem, rsem, peer):
        return send(src.at[peer], dst.at[me], ssem.at[peer], rsem.at[me], {"tracer": peer})

    def scatter_wait(src, dst, ssem, rsem):
        for peer in others:
            send(src.at[peer], dst.at[peer], ssem.at[peer], rsem.at[peer], {"tracer": peer}).wait_recv()

    for peer in others:
        scatter(pqs, pqr, pqss, pqrs, peer).start()
    gather_start(fa, fas, far)
    for c in y_copies(0):
        c.start()

    def x_start(s, j):
        up, down = x_copies(s, j)
        pl.when(has_hi)(up.start)
        pl.when(has_lo)(down.start)

    for j in range(nt):
        x_start(0, j)

    c_right.wait_recv()
    c_left.wait_recv()
    pl.when(has_hi)(c_down.wait_recv)

    @pl.when(has_lo)
    def _():
        c_up.wait_recv()

    @pl.when(gx == 0)
    def _():
        for k in range(3):
            cxl[k] = zero

    @pl.when(gx == nx - 1)
    def _():
        cxh[0] = zero

    fb[me, 0] = cxl[2]
    fb[me, 1] = cyl[2]
    gather_start(fb, fbs, fbr)

    for k in range(2 * own):
        pqr[me, k] = pqs[me, k]
    scatter_wait(pqs, pqr, pqss, pqrs)
    scale = 4.0 / total
    for b in range(own):
        prey = pqr[0, b]
        sq = pqr[0, own + b]
        for j in range(1, nt):
            prey = prey + pqr[j, b]
            sq = sq + pqr[j, own + b]
        f1[me, b] = gzv[me * own + b] / (1.0 + scale * prey)
        own1[b] = sq
    gather_start(f1, f1s, f1r)

    dep_l = cyl[0] * (gy > 0).astype(F32)
    dep_r = cyh[0] * (gy < ny - 1).astype(F32)
    dep_m = cys[0]
    plevf = plev.astype(F32)
    wet0 = (plevf < jnp.where(e < 2, dep_l, dep_m)).astype(F32)
    wet1 = (plevf < jnp.where(e < 2, dep_m, dep_r)).astype(F32)
    open0 = wet0 * roll(wet0, 1)
    open1 = wet1 * roll(wet1, 1)
    wx[...] = jnp.zeros_like(wx)
    wx[pl.ds(LO, 2), :] = cxl[0, pl.ds(6, 2), :]
    wx[pl.ds(IN, 8), :] = depth
    wx[pl.ds(HI, 2), :] = cxh[0, pl.ds(0, 2), :]
    gather_wait(fa, fas, far)
    flux_edge = fa[0, 3 * own]
    for j in range(1, nt):
        flux_edge = flux_edge + fa[j, 3 * own]
    ec[0] = 0.5 * open0
    ec[2] = 2.0 * open0 * roll(cyl[1], 1)
    ec[3] = 0.5 * open1
    ec[4] = flux_edge * open1
    ec[5] = 2.0 * open1 * roll(cys[1], 1)
    dn_low = 2.0 * roll(dnv[...], 1)
    depth_y = jnp.minimum(depth, roll(depth, 1))

    for l in range(lev):
        j, b = l // own, l % own
        open_y = (depth_y > l).astype(F32)
        hy[l] = 0.5 * open_y
        fy[l] = roll(fa[j, own + b], 1) * open_y
        ky[l] = dn_low * open_y
        if l:
            open_z = (depth > l).astype(F32)
            hz[l] = 0.5 * open_z
            fz[l] = fa[(l - 1) // own, 2 * own + (l - 1) % own] * open_z
        fx[l, pl.ds(IN, 8), :] = fa[j, b]

    def edge(cells, h, flux, kappa):
        below = roll(cells, 1)
        jump = h * (cells - below)
        slope = minmod(jump, roll(jump, -1))
        carried = flux * jnp.where(flux > 0.0, below + roll(slope, 1), cells - slope) - kappa * jump
        return jump, carried

    def y_edges(s):
        for c in y_copies(s):
            c.wait_recv()
        for p in range(t_dev // 2):
            mine = yp[s, p]
            j0, c0 = edge(jnp.where(e < 2, yl[s, p], mine), ec[0], ec[1], ec[2])
            j1, c1 = edge(jnp.where(e < 2, mine, yr[s, p]), ec[3], ec[4], ec[5])
            g1[p] = jnp.where(e == 0, roll(j1, -2), roll(j0, -1))
            g2[p] = jnp.where(e == 0, roll(c1, -2), roll(c0, -1))

    def yz_part(s):
        def pair(p, carry):
            for h in range(2):
                t = 2 * p + h
                cells = [ext[s, t, l, pl.ds(IN, 8), :] for l in range(lev)]
                jumps = [zero] + [hz[l] * (cells[l] - cells[l - 1]) for l in range(1, lev)] + [zero]
                slopes = [minmod(jumps[l], jumps[l + 1]) for l in range(lev)]
                faces = [zero]
                for l in range(1, lev):
                    f = fz[l]
                    faces.append(f * jnp.where(f > 0.0, cells[l - 1] + slopes[l - 1], cells[l] - slopes[l]))
                faces.append(zero)
                for l in range(lev):
                    q = h * lev + l
                    c = cells[l]
                    e1 = roll(g1[p], -(4 * q + 1))
                    e2 = roll(g2[p], -(4 * q + 1))
                    below = roll(c, 1)
                    f = fy[l]
                    jump = jnp.where(lane0, e1, hy[l] * (c - below))
                    jump_up = jnp.where(lane127, e1, roll(jump, -1))
                    slope = minmod(jump, jump_up)
                    carried = f * jnp.where(f > 0.0, below + roll(slope, 1), c - slope) - ky[l] * jump
                    carried = jnp.where(lane0, e2, carried)
                    carried_up = jnp.where(lane127, e2, roll(carried, -1))
                    adv[t, l] = c + ((carried - carried_up) + (faces[l] - faces[l + 1]))
            return carry

        lax.fori_loop(0, t_dev // 2, pair, 0)

    def x_part(s, reduce_r):
        def chunk(j, carry):
            up, down = x_copies(s, j)
            pl.when(has_lo)(up.wait_recv)
            pl.when(has_hi)(down.wait_recv)
            for b in range(own):
                l = j * own + b
                h = [hx[l, pl.ds(IN - 1 + k, 8), :] for k in range(4)]
                f = [fx[l, pl.ds(IN - 1 + k, 8), :] for k in range(2)]
                kk = [kx[l, pl.ds(IN + k, 8), :] for k in range(2)]
                total_r = zero
                for t in range(t_dev):
                    ext[s, t, l, pl.ds(LO, 2), :] = xl[s, l, pl.ds(2 * t, 2), :]
                    ext[s, t, l, pl.ds(HI, 2), :] = xh[s, l, pl.ds(2 * t, 2), :]
                    c = [ext[s, t, l, pl.ds(LO + k, 8), :] for k in range(5)]
                    jump = [h[k] * (c[k + 1] - c[k]) for k in range(4)]
                    slope = [minmod(jump[k], jump[k + 1]) for k in range(3)]
                    carried = [
                        f[k] * jnp.where(f[k] > 0.0, c[k + 1] + slope[k], c[k + 2] - slope[k + 1])
                        - kk[k] * jump[k + 1]
                        for k in range(2)
                    ]
                    a = adv[t, l] + (carried[0] - carried[1])
                    adv[t, l] = a
                    if reduce_r:
                        total_r = total_r + tv[t] * a
                if reduce_r:
                    rs[j, b] = total_r
            if reduce_r:
                @pl.when(j != me)
                def _():
                    scatter(rs, rr, rss, rrs, j).start()
            return carry

        lax.fori_loop(0, nt, chunk, 0)

    for s in range(STEPS):
        @pl.when(gx == 0)
        def _():
            xl[s] = jnp.zeros_like(xl[s])

        @pl.when(gx == nx - 1)
        def _():
            xh[s] = jnp.zeros_like(xh[s])

    gather_wait(fb, fbs, fbr)
    flux_edge = fb[0, 1]
    for j in range(1, nt):
        flux_edge = flux_edge + fb[j, 1]
    ec[1] = flux_edge * open0
    for l in range(lev):
        fx[l, pl.ds(IN - 1, 1), :] = fb[l // own, 0, pl.ds(l % own, 1), :]
    d_low = jnp.concatenate([2.0 * cxl[1, pl.ds(7, 1), :], 2.0 * dev[pl.ds(0, 7), :]], axis=0)
    d_up = 2.0 * dev[...]
    depth_x = [
        jnp.minimum(wx[pl.ds(LO + k, 8), :], wx[pl.ds(LO + 1 + k, 8), :]) for k in range(4)
    ]
    for l in range(lev):
        opens = [(depth_x[k] > l).astype(F32) for k in range(4)]
        low = fx[l, pl.ds(IN - 1, 8), :] * opens[1]
        up = fx[l, pl.ds(IN, 8), :] * opens[2]
        hx[l, pl.ds(IN - 1, 8), :] = 0.5 * opens[0]
        hx[l, pl.ds(IN + 2, 8), :] = 0.5 * opens[3]
        fx[l, pl.ds(IN - 1, 8), :] = low
        fx[l, pl.ds(IN, 8), :] = up
        kx[l, pl.ds(IN, 8), :] = d_low * opens[1]
        kx[l, pl.ds(IN + 1, 8), :] = d_up * opens[2]

    y_edges(0)
    yz_part(0)
    x_part(0, True)
    gather_wait(f1, f1s, f1r)

    def second(l, acc):
        j, b = l // own, lax.rem(l, own)
        factor = f1[j, b]
        tiles = []
        for t in range(t_dev):
            c = adv[t, l] - (tv[t] * factor) * ext[0, t, l, pl.ds(IN, 8), :]
            ext[1, t, l, pl.ds(IN, 8), :] = c
            tiles.append(c)
        return pack_level(1, l, tiles, acc)

    acc = lax.fori_loop(0, lev, second, tuple(zero for _ in range(t_dev // 2)))
    for p in range(t_dev // 2):
        yp[1, p] = acc[p]
    for c in y_copies(1):
        c.start()
    for j in range(nt):
        x_start(1, j)

    for b in range(own):
        rr[me, b] = rs[me, b]
    scatter_wait(rs, rr, rss, rrs)
    for b in range(own):
        prey = rr[0, b]
        for j in range(1, nt):
            prey = prey + rr[j, b]
        prey = prey - f1[me, b] * own1[b]
        f2[me, b] = gzv[me * own + b] / (1.0 + scale * prey)
    gather_start(f2, f2s, f2r)

    y_edges(1)
    yz_part(1)
    x_part(1, False)
    gather_wait(f2, f2s, f2r)

    def last(l, carry):
        j, b = l // own, lax.rem(l, own)
        factor = f2[j, b]
        for t in range(t_dev):
            outv[t, l] = adv[t, l] - (tv[t] * factor) * ext[1, t, l, pl.ds(IN, 8), :]
        return carry

    lax.fori_loop(0, lev, last, 0)
    store = pltpu.make_async_copy(outv, out, osem)
    store.start()

    c_right.wait_send()
    c_left.wait_send()
    pl.when(has_hi)(c_up.wait_send)
    pl.when(has_lo)(c_down.wait_send)
    for s in range(STEPS):
        for c in y_copies(s):
            c.wait_send()
        for j in range(nt):
            up, down = x_copies(s, j)
            pl.when(has_hi)(up.wait_send)
            pl.when(has_lo)(down.wait_send)
    gather_done(fa, fas, far)
    gather_done(fb, fbs, fbr)
    gather_done(f1, f1s, f1r)
    gather_done(f2, f2s, f2r)
    for peer in others:
        scatter(pqs, pqr, pqss, pqrs, peer).wait_send()
        scatter(rs, rr, rss, rrs, peer).wait_send()
    store.wait()


def on_device(tracers, fluxes, diff_east, diff_north, column_depth, grazers, groups, preference):
    t_dev, lev, rows, cols = tracers.shape
    nt, nx, ny = (lax.axis_size(a) for a in ("tracer", "gx", "gy"))
    own = lev // nt
    tile = (8, LANES)
    half = t_dev // 2
    dma = pltpu.SemaphoreType.DMA

    def v(*shape):
        return pltpu.VMEM(shape, F32)

    scratch = [
        v(2, t_dev, lev, 24, LANES), v(t_dev, lev, *tile), v(t_dev, lev, *tile),
        v(3, own, *tile), v(*tile), v(*tile), pltpu.VMEM(tile, jnp.int32), v(lev, *tile),
        pltpu.SMEM(groups.shape, jnp.int32), pltpu.SMEM(preference.shape, F32), v(t_dev, *tile),
        v(3, *tile), v(3, *tile), v(1, *tile), v(3, *tile), v(3, *tile), v(1, *tile),
        v(nt, 3 * own + 1, *tile), v(nt, 2, *tile), v(lev, 24, LANES),
        v(nt, 2 * own, *tile), v(nt, 2 * own, *tile), v(nt, own, *tile), v(nt, own, *tile),
        v(nt, own, *tile), v(nt, own, *tile), v(own, *tile),
        v(2, lev, 2 * t_dev, LANES), v(2, lev, 2 * t_dev, LANES),
        v(2, lev, 2 * t_dev, LANES), v(2, lev, 2 * t_dev, LANES),
        v(2, half, *tile), v(2, half, *tile), v(2, half, *tile), v(half, *tile), v(half, *tile),
        v(lev, *tile), v(lev, *tile), v(lev, *tile), v(lev, *tile), v(lev, *tile),
        v(lev, 24, LANES), v(lev, 24, LANES), v(24, LANES), v(6, *tile),
        dma((8,)), dma((4,)), dma((4,)),
        dma((nt,)), dma((nt,)), dma((nt,)), dma((nt,)), dma((nt,)), dma((nt,)),
        dma((nt,)), dma((nt,)), dma((nt,)), dma((nt,)), dma((nt,)), dma((nt,)),
        dma((2, 2, nt)), dma((2, 2, nt)), dma((2, 2)), dma((2, 2)), dma,
    ]
    return pl.pallas_call(
        functools.partial(kernel, (nt, nx, ny, t_dev, lev, t_dev * nt)),
        out_shape=jax.ShapeDtypeStruct(tracers.shape, F32),
        in_specs=[pl.BlockSpec(memory_space=pl.ANY)] * 8,
        out_specs=pl.BlockSpec(memory_space=pl.ANY),
        scratch_shapes=scratch,
        compiler_params=pltpu.CompilerParams(collective_id=0, has_side_effects=True),
        name="plankton",
    )(tracers, fluxes, diff_east, diff_north, column_depth, grazers, groups, preference)


def solution(mesh):
    placed = (
        P("tracer", None, "gx", "gy"),
        P(None, "tracer", "gx", "gy"),
        P("gx", "gy"),
        P("gx", "gy"),
        P("gx", "gy"),
        P(None, "gx", "gy"),
        P("tracer"),
        P(),
    )
    return jax.shard_map(
        on_device,
        mesh=mesh,
        in_specs=placed,
        out_specs=P("tracer", None, "gx", "gy"),
        check_vma=False,
    )
```

```python
import functools

import jax
import jax.numpy as jnp
from jax import lax
from jax.experimental import pallas as pl
from jax.experimental.pallas import tpu as pltpu
from jax.sharding import PartitionSpec as P

STEPS = 2
MESH = pl.DeviceIdType.MESH
F32 = jnp.float32
LANES = 128
LO, IN, HI = 6, 8, 16


def minmod(a, b):
    return jnp.maximum(0.0, jnp.minimum(a, b)) + jnp.minimum(0.0, jnp.maximum(a, b))


def roll(v, shift):
    return pltpu.roll(v, shift % LANES, 1)


def kernel(
    dims, tr, fl, de, dn, dep, gz, grp, prf, adv, grazed, f2,
    ext, flv, dev, dnv, depv, gzv, grps, prfs, tv,
    cxs, cxl, cxh, cys, cyl, cyh, fa, fb, fx,
    pqs, pqr, rs, rr, f1, own1,
    sxl, sxh, xl, xh, yp, yl, yr, ge, yst, gsl, gsh, gxl, gxh, tx,
    hy, fy, ky, hz, fz, hx, kx, wx, ec,
    lsem, csem, crec, fas, far, fbs, fbr, pqss, pqrs, rss, rrs, f1s, f1r, f2s, f2r,
    xss, xrs, yss, yrs, gss, grs,
):
    nt, nx, ny, t_dev, lev, total = dims
    own = lev // nt
    me, gx, gy = lax.axis_index("tracer"), lax.axis_index("gx"), lax.axis_index("gy")
    left, right = lax.rem(gy + ny - 1, ny), lax.rem(gy + 1, ny)
    has_lo, has_hi = gx > 0, gx < nx - 1
    others = [lax.rem(me + d, nt) for d in range(1, nt)]

    loads = [
        (tr, ext.at[0, :, :, pl.ds(IN, 8), :]), (fl, flv), (de, dev), (dn, dnv), (dep, depv),
        (gz, gzv), (grp, grps), (prf, prfs),
    ]
    loads = [pltpu.make_async_copy(a, b, lsem.at[i]) for i, (a, b) in enumerate(loads)]

    barrier = pltpu.get_barrier_semaphore()
    for peer in others:
        pl.semaphore_signal(barrier, inc=1, device_id={"tracer": peer}, device_id_type=MESH)
    for z in (left, right):
        pl.semaphore_signal(barrier, inc=1, device_id={"gy": z}, device_id_type=MESH)

    @pl.when(has_lo)
    def _():
        pl.semaphore_signal(barrier, inc=1, device_id={"gx": gx - 1}, device_id_type=MESH)

    @pl.when(has_hi)
    def _():
        pl.semaphore_signal(barrier, inc=1, device_id={"gx": gx + 1}, device_id_type=MESH)

    for c in loads:
        c.start()

    lane = lax.broadcasted_iota(jnp.int32, (8, LANES), 1)
    row = lax.broadcasted_iota(jnp.int32, (8, LANES), 0)
    plev, e = lane // 8, lane % 8
    at_edge = (lane < 2) | (lane >= LANES - 2)
    zero = jnp.zeros((8, LANES), F32)

    def spread(v):
        base = jnp.where(lane < 8, roll(v, 4), zero)
        for s in (8, 16, 32, 64):
            base = base + roll(base, s)
        return base

    for c in loads[1:]:
        c.wait()
    for t in range(t_dev):
        w = jnp.full((8, LANES), prfs[grps[t]], F32)
        tv[t] = w
        tx[t // 4] = w if t % 4 == 0 else jnp.where(row // 2 == t % 4, w, tx[t // 4])
    depth = depv[...].astype(F32)
    cxs[0] = depth
    cxs[1] = dev[...]
    rows_tile = zero
    lanes_tile = zero
    for b in range(own):
        rows_tile = jnp.where(row == b, flv[0, b, pl.ds(7, 1), :], rows_tile)
        lanes_tile = jnp.where(plev == me * own + b, spread(flv[1, b]), lanes_tile)
    cxs[2] = rows_tile
    cys[0] = spread(depth)
    cys[1] = spread(dnv[...])
    cys[2] = lanes_tile
    for k in range(3):
        for b in range(own):
            fa[me, k * own + b] = flv[k, b]
    fa[me, 3 * own] = lanes_tile
    loads[0].wait()

    def send(src, dst, ssem, rsem, to):
        return pltpu.make_async_remote_copy(
            src_ref=src, dst_ref=dst, send_sem=ssem, recv_sem=rsem, device_id=to, device_id_type=MESH
        )

    def pack_level(s, l, tiles, acc):
        acc = list(acc)
        for t in range(t_dev):
            if s == 0:
                sxl[s, l, pl.ds(2 * t, 2), :] = ext[s, t, l, pl.ds(IN, 2), :]
                sxh[s, l, pl.ds(2 * t, 2), :] = ext[s, t, l, pl.ds(IN + 6, 2), :]
            acc[t] = jnp.where(plev == l, pltpu.roll(tiles[t], 8 * l + 4, 1), acc[t])
        return tuple(acc)

    def first(l, acc):
        tiles = [ext[0, t, l, pl.ds(IN, 8), :] for t in range(t_dev)]
        p_sum, q_sum = zero, zero
        for t in range(t_dev):
            w = tv[t]
            wc = w * tiles[t]
            p_sum = p_sum + wc
            q_sum = q_sum + w * wc
        j, b = l // own, lax.rem(l, own)
        pqs[j, b] = p_sum
        pqs[j, own + b] = q_sum
        return pack_level(0, l, tiles, acc)

    acc = lax.fori_loop(0, lev, first, tuple(zero for _ in range(t_dev)))
    for t in range(t_dev):
        yp[0, t] = acc[t]

    pl.semaphore_wait(barrier, nt - 1 + 2 + has_lo.astype(jnp.int32) + has_hi.astype(jnp.int32))

    c_right = send(cys, cyl, csem.at[0], crec.at[0], {"gy": right})
    c_left = send(cys.at[pl.ds(0, 1)], cyh, csem.at[1], crec.at[1], {"gy": left})
    c_up = send(cxs, cxl, csem.at[2], crec.at[2], {"gx": gx + 1})
    c_down = send(cxs.at[pl.ds(0, 1)], cxh, csem.at[3], crec.at[3], {"gx": gx - 1})
    c_right.start()
    c_left.start()
    pl.when(has_hi)(c_up.start)
    pl.when(has_lo)(c_down.start)

    def y_copies(s):
        return (
            send(yp.at[s], yl.at[s], yss.at[s, 0], yrs.at[s, 0], {"gy": right}),
            send(yp.at[s], yr.at[s], yss.at[s, 1], yrs.at[s, 1], {"gy": left}),
        )

    def x_copies(s, j):
        c = pl.ds(j * own, own)
        return (
            send(sxh.at[s, c], xl.at[s, c], xss.at[s, 0, j], xrs.at[s, 0, j], {"gx": gx + 1}),
            send(sxl.at[s, c], xh.at[s, c], xss.at[s, 1, j], xrs.at[s, 1, j], {"gx": gx - 1}),
        )

    def gather_start(buf, ssem, rsem):
        for d, peer in enumerate(others):
            send(buf.at[me], buf.at[me], ssem.at[d], rsem.at[me], {"tracer": peer}).start()

    def gather_wait(buf, ssem, rsem):
        for d, peer in enumerate(others):
            send(buf.at[me], buf.at[peer], ssem.at[d], rsem.at[peer], {"tracer": peer}).wait_recv()

    def gather_done(buf, ssem, rsem):
        for d, peer in enumerate(others):
            send(buf.at[me], buf.at[peer], ssem.at[d], rsem.at[peer], {"tracer": peer}).wait_send()

    def scatter(src, dst, ssem, rsem, peer):
        return send(src.at[peer], dst.at[me], ssem.at[peer], rsem.at[me], {"tracer": peer})

    def scatter_wait(src, dst, ssem, rsem):
        for peer in others:
            send(src.at[peer], dst.at[peer], ssem.at[peer], rsem.at[peer], {"tracer": peer}).wait_recv()

    for peer in others:
        scatter(pqs, pqr, pqss, pqrs, peer).start()
    gather_start(fa, fas, far)
    for c in y_copies(0):
        c.start()

    def x_start(s, j):
        up, down = x_copies(s, j)
        pl.when(has_hi)(up.start)
        pl.when(has_lo)(down.start)

    for j in range(nt):
        x_start(0, j)

    c_right.wait_recv()
    c_left.wait_recv()
    pl.when(has_hi)(c_down.wait_recv)

    @pl.when(has_lo)
    def _():
        c_up.wait_recv()

    @pl.when(gx == 0)
    def _():
        for k in range(3):
            cxl[k] = zero

    @pl.when(gx == nx - 1)
    def _():
        cxh[0] = zero

    fb[me, 0] = cxl[2]
    fb[me, 1] = cyl[2]
    gather_start(fb, fbs, fbr)

    dep_l = cyl[0] * (gy > 0).astype(F32)
    dep_r = cyh[0] * (gy < ny - 1).astype(F32)
    dep_m = cys[0]
    plevf = plev.astype(F32)
    wet0 = (plevf < jnp.where(e < 4, dep_l, dep_m)).astype(F32)
    wet1 = (plevf < jnp.where(e < 4, dep_m, dep_r)).astype(F32)
    open0 = wet0 * roll(wet0, 1)
    open1 = wet1 * roll(wet1, 1)
    wx[...] = jnp.zeros_like(wx)
    wx[pl.ds(LO, 2), :] = cxl[0, pl.ds(6, 2), :]
    wx[pl.ds(IN, 8), :] = depth
    wx[pl.ds(HI, 2), :] = cxh[0, pl.ds(0, 2), :]
    for k in range(2 * own):
        pqr[me, k] = pqs[me, k]
    scatter_wait(pqs, pqr, pqss, pqrs)
    scale = 4.0 / total
    for b in range(own):
        prey = pqr[0, b]
        sq = pqr[0, own + b]
        for j in range(1, nt):
            prey = prey + pqr[j, b]
            sq = sq + pqr[j, own + b]
        f1[me, b] = gzv[me * own + b] / (1.0 + scale * prey)
        own1[b] = sq
    gather_start(f1, f1s, f1r)

    gather_wait(fa, fas, far)
    flux_edge = fa[0, 3 * own]
    for j in range(1, nt):
        flux_edge = flux_edge + fa[j, 3 * own]
    ec[0] = 0.5 * open0
    ec[1] = flux_edge
    ec[2] = 2.0 * open0 * roll(jnp.where(e < 4, cyl[1], cys[1]), 1)
    ec[3] = 0.5 * open1
    ec[4] = roll(flux_edge, 1) * open1
    ec[5] = 2.0 * open1 * roll(cys[1], 1)
    dn_low = 2.0 * roll(dnv[...], 1)
    depth_y = jnp.minimum(depth, roll(depth, 1))

    for l in range(lev):
        j, b = l // own, l % own
        open_y = (depth_y > l).astype(F32)
        hy[l] = 0.5 * open_y
        fy[l] = roll(fa[j, own + b], 1) * open_y
        ky[l] = dn_low * open_y
        if l:
            open_z = (depth > l).astype(F32)
            hz[l] = 0.5 * open_z
            fz[l] = fa[(l - 1) // own, 2 * own + (l - 1) % own] * open_z
        fx[l, pl.ds(IN, 8), :] = fa[j, b]

    def edge(cells, h, flux, kappa):
        below = roll(cells, 1)
        jump = h * (cells - below)
        slope = minmod(jump, roll(jump, -1))
        carried = flux * jnp.where(flux > 0.0, below + roll(slope, 1), cells - slope) - kappa * jump
        return carried - roll(carried, -1)

    def y_edges(s):
        for c in y_copies(s):
            c.wait_recv()
        for t in range(t_dev):
            mine = yp[s, t]
            low = edge(jnp.where(e < 4, yl[s, t], mine), ec[0], ec[1], ec[2])
            high = edge(jnp.where(e < 4, mine, yr[s, t]), ec[3], ec[4], ec[5])
            ge[t] = jnp.where(e < 4, high, low)

    def z_part(s):
        def pair(p, carry):
            for h in range(2):
                t = 2 * p + h
                cells = [ext[s, t, l, pl.ds(IN, 8), :] for l in range(lev)]
                jumps = [zero] + [hz[l] * (cells[l] - cells[l - 1]) for l in range(1, lev)] + [zero]
                slopes = [minmod(jumps[l], jumps[l + 1]) for l in range(lev)]
                faces = [zero]
                for l in range(1, lev):
                    f = fz[l]
                    faces.append(f * jnp.where(f > 0.0, cells[l - 1] + slopes[l - 1], cells[l] - slopes[l]))
                faces.append(zero)
                for l in range(lev):
                    adv[t, l] = cells[l] + (faces[l] - faces[l + 1])
            return carry

        lax.fori_loop(0, t_dev // 2, pair, 0)

    def y_part(s):
        def slopes(l, slot):
            h = hy[l]
            h_up = roll(h, -1)
            for t in range(t_dev):
                c = ext[s, t, l, pl.ds(IN, 8), :]
                jump = h * (c - roll(c, 1))
                jump_up = h_up * (roll(c, -1) - c)
                slope = minmod(jump, jump_up)
                yst[slot, 0, t] = c + slope
                yst[slot, 1, t] = c - slope
                yst[slot, 2, t] = jump
                yst[slot, 3, t] = jump_up

        def fluxes(l, slot):
            f, k = fy[l], ky[l]
            f_up, k_up = roll(f, -1), roll(k, -1)
            ahead, ahead_up = f > 0.0, f_up > 0.0
            for t in range(t_dev):
                fore, aft = yst[slot, 0, t], yst[slot, 1, t]
                carried = f * jnp.where(ahead, roll(fore, 1), aft) - k * yst[slot, 2, t]
                carried_up = f_up * jnp.where(ahead_up, fore, roll(aft, -1)) - k_up * yst[slot, 3, t]
                outer = pltpu.roll(ge[t], (LANES - 4) - 8 * l, 1)
                adv[t, l] = adv[t, l] + jnp.where(at_edge, outer, carried - carried_up)

        def level(l, carry):
            slopes(l, lax.rem(l, 2))
            fluxes(l - 1, lax.rem(l + 1, 2))
            return carry

        slopes(0, 0)
        lax.fori_loop(1, lev, level, 0)
        fluxes(lev - 1, (lev - 1) % 2)

    def x_part(s):
        def chunk(j, carry):
            up, down = x_copies(s, j)
            pl.when(has_lo)(up.wait_recv)
            pl.when(has_hi)(down.wait_recv)
            for b in range(own):
                l = j * own + b
                if s:
                    for halo, fac in ((xl, gxl), (xh, gxh)):
                        two = pl.multiple_of(2 * l, 2)
                        f8 = jnp.where(row % 2 == 0, fac[pl.ds(two, 1), :], fac[pl.ds(two + 1, 1), :])
                        for k in range(2 * t_dev // 8):
                            r = pl.ds(8 * k, 8)
                            halo[1, l, r, :] = halo[1, l, r, :] - (tx[k] * f8) * halo[0, l, r, :]
                h = [hx[l, pl.ds(IN - 1 + k, 8), :] for k in range(4)]
                f = [fx[l, pl.ds(IN - 1 + k, 8), :] for k in range(2)]
                kk = [kx[l, pl.ds(IN + k, 8), :] for k in range(2)]
                ahead = [f[k] > 0.0 for k in range(2)]
                total_r = zero
                for t in range(t_dev):
                    two = pl.ds(2 * t, 2)
                    ext[s, t, l, pl.ds(LO, 2), :] = xl[s, l, two, :]
                    ext[s, t, l, pl.ds(HI, 2), :] = xh[s, l, two, :]
                    c = [ext[s, t, l, pl.ds(LO + k, 8), :] for k in range(5)]
                    jump = [h[k] * (c[k + 1] - c[k]) for k in range(4)]
                    slope = [minmod(jump[k], jump[k + 1]) for k in range(3)]
                    carried = [
                        f[k] * jnp.where(ahead[k], c[k + 1] + slope[k], c[k + 2] - slope[k + 1])
                        - kk[k] * jump[k + 1]
                        for k in range(2)
                    ]
                    a = adv[t, l] + (carried[0] - carried[1])
                    adv[t, l] = a
                    if s == 0:
                        total_r = total_r + tv[t] * a
                        sxl[1, l, two, :] = adv[t, l, pl.ds(0, 2), :]
                        sxh[1, l, two, :] = adv[t, l, pl.ds(6, 2), :]
                if s == 0:
                    rs[j, b] = total_r
            if s == 0:
                @pl.when(j != me)
                def _():
                    scatter(rs, rr, rss, rrs, j).start()

                x_start(1, j)
            return carry

        lax.fori_loop(0, nt, chunk, 0)

    for s in range(STEPS):
        @pl.when(gx == 0)
        def _():
            xl[s] = jnp.zeros_like(xl[s])

        @pl.when(gx == nx - 1)
        def _():
            xh[s] = jnp.zeros_like(xh[s])

    gather_wait(fb, fbs, fbr)
    flux_edge = fb[0, 1]
    for j in range(1, nt):
        flux_edge = flux_edge + fb[j, 1]
    ec[1] = roll(jnp.where(e < 4, flux_edge, ec[1]), 1) * open0
    for l in range(lev):
        fx[l, pl.ds(IN - 1, 1), :] = fb[l // own, 0, pl.ds(l % own, 1), :]
    d_low = jnp.concatenate([2.0 * cxl[1, pl.ds(7, 1), :], 2.0 * dev[pl.ds(0, 7), :]], axis=0)
    d_up = 2.0 * dev[...]
    depth_x = [
        jnp.minimum(wx[pl.ds(LO + k, 8), :], wx[pl.ds(LO + 1 + k, 8), :]) for k in range(4)
    ]
    for l in range(lev):
        opens = [(depth_x[k] > l).astype(F32) for k in range(4)]
        low = fx[l, pl.ds(IN - 1, 8), :] * opens[1]
        up = fx[l, pl.ds(IN, 8), :] * opens[2]
        hx[l, pl.ds(IN - 1, 8), :] = 0.5 * opens[0]
        hx[l, pl.ds(IN + 2, 8), :] = 0.5 * opens[3]
        fx[l, pl.ds(IN - 1, 8), :] = low
        fx[l, pl.ds(IN, 8), :] = up
        kx[l, pl.ds(IN, 8), :] = d_low * opens[1]
        kx[l, pl.ds(IN + 1, 8), :] = d_up * opens[2]

    z_part(0)
    y_edges(0)
    y_part(0)
    x_part(0)
    gather_wait(f1, f1s, f1r)
    for l in range(lev):
        gsl[pl.ds(2 * l, 2), :] = f1[l // own, l % own, pl.ds(0, 2), :]
        gsh[pl.ds(2 * l, 2), :] = f1[l // own, l % own, pl.ds(6, 2), :]
    g_up = send(gsh, gxl, gss.at[0], grs.at[0], {"gx": gx + 1})
    g_down = send(gsl, gxh, gss.at[1], grs.at[1], {"gx": gx - 1})
    pl.when(has_hi)(g_up.start)
    pl.when(has_lo)(g_down.start)

    def second(l, acc):
        j, b = l // own, lax.rem(l, own)
        factor = f1[j, b]
        tiles = []
        for t in range(t_dev):
            c = adv[t, l] - (tv[t] * factor) * ext[0, t, l, pl.ds(IN, 8), :]
            ext[1, t, l, pl.ds(IN, 8), :] = c
            grazed[t, l] = tv[t] * c
            tiles.append(c)
        return pack_level(1, l, tiles, acc)

    acc = lax.fori_loop(0, lev, second, tuple(zero for _ in range(t_dev)))
    for t in range(t_dev):
        yp[1, t] = acc[t]
    for c in y_copies(1):
        c.start()
    z_part(1)

    for b in range(own):
        rr[me, b] = rs[me, b]
    scatter_wait(rs, rr, rss, rrs)
    for b in range(own):
        prey = rr[0, b]
        for j in range(1, nt):
            prey = prey + rr[j, b]
        prey = prey - f1[me, b] * own1[b]
        f2[me, b] = gzv[me * own + b] / (1.0 + scale * prey)
    gather_start(f2, f2s, f2r)

    y_edges(1)
    y_part(1)
    pl.when(has_lo)(g_up.wait_recv)
    pl.when(has_hi)(g_down.wait_recv)

    @pl.when(gx == 0)
    def _():
        gxl[...] = jnp.zeros_like(gxl)

    @pl.when(gx == nx - 1)
    def _():
        gxh[...] = jnp.zeros_like(gxh)

    x_part(1)
    gather_wait(f2, f2s, f2r)

    c_right.wait_send()
    c_left.wait_send()
    pl.when(has_hi)(c_up.wait_send)
    pl.when(has_lo)(c_down.wait_send)
    pl.when(has_hi)(g_up.wait_send)
    pl.when(has_lo)(g_down.wait_send)
    for s in range(STEPS):
        for c in y_copies(s):
            c.wait_send()
        for j in range(nt):
            up, down = x_copies(s, j)
            pl.when(has_hi)(up.wait_send)
            pl.when(has_lo)(down.wait_send)
    gather_done(fa, fas, far)
    gather_done(fb, fbs, fbr)
    gather_done(f1, f1s, f1r)
    gather_done(f2, f2s, f2r)
    for peer in others:
        scatter(pqs, pqr, pqss, pqrs, peer).wait_send()
        scatter(rs, rr, rss, rrs, peer).wait_send()


def on_device(tracers, fluxes, diff_east, diff_north, column_depth, grazers, groups, preference):
    t_dev, lev, rows, cols = tracers.shape
    nt, nx, ny = (lax.axis_size(a) for a in ("tracer", "gx", "gy"))
    own = lev // nt
    tile = (8, LANES)
    dma = pltpu.SemaphoreType.DMA

    def v(*shape):
        return pltpu.VMEM(shape, F32)

    scratch = [
        v(2, t_dev, lev, 24, LANES),
        v(3, own, *tile), v(*tile), v(*tile), pltpu.VMEM(tile, jnp.int32), v(lev, *tile),
        pltpu.SMEM(groups.shape, jnp.int32), pltpu.SMEM(preference.shape, F32), v(t_dev, *tile),
        v(3, *tile), v(3, *tile), v(1, *tile), v(3, *tile), v(3, *tile), v(1, *tile),
        v(nt, 3 * own + 1, *tile), v(nt, 2, *tile), v(lev, 24, LANES),
        v(nt, 2 * own, *tile), v(nt, 2 * own, *tile), v(nt, own, *tile), v(nt, own, *tile),
        v(nt, own, *tile), v(own, *tile),
        v(2, lev, 2 * t_dev, LANES), v(2, lev, 2 * t_dev, LANES),
        v(2, lev, 2 * t_dev, LANES), v(2, lev, 2 * t_dev, LANES),
        v(2, t_dev, *tile), v(2, t_dev, *tile), v(2, t_dev, *tile), v(t_dev, *tile), v(2, 4, t_dev, *tile),
        v(2 * lev, LANES), v(2 * lev, LANES), v(2 * lev, LANES), v(2 * lev, LANES), v(2 * t_dev // 8, *tile),
        v(lev, *tile), v(lev, *tile), v(lev, *tile), v(lev, *tile), v(lev, *tile),
        v(lev, 24, LANES), v(lev, 24, LANES), v(24, LANES), v(6, *tile),
        dma((8,)), dma((4,)), dma((4,)),
        dma((nt,)), dma((nt,)), dma((nt,)), dma((nt,)), dma((nt,)), dma((nt,)),
        dma((nt,)), dma((nt,)), dma((nt,)), dma((nt,)), dma((nt,)), dma((nt,)),
        dma((2, 2, nt)), dma((2, 2, nt)), dma((2, 2)), dma((2, 2)), dma((2,)), dma((2,)),
    ]
    moved, grazed, factor = pl.pallas_call(
        functools.partial(kernel, (nt, nx, ny, t_dev, lev, t_dev * nt)),
        out_shape=(
            jax.ShapeDtypeStruct(tracers.shape, F32),
            jax.ShapeDtypeStruct(tracers.shape, F32),
            jax.ShapeDtypeStruct((nt, own, *tile), F32),
        ),
        in_specs=[pl.BlockSpec(memory_space=pltpu.HBM)] * 8,
        out_specs=[pl.BlockSpec(memory_space=pltpu.VMEM)] * 3,
        scratch_shapes=scratch,
        compiler_params=pltpu.CompilerParams(
            collective_id=0, has_side_effects=True, vmem_limit_bytes=20 * 1024 * 1024
        ),
        name="plankton",
    )(*[
        pltpu.with_memory_space_constraint(a, pltpu.HBM)
        for a in (tracers, fluxes, diff_east, diff_north, column_depth, grazers, groups, preference)
    ])
    return moved - factor.reshape(lev, *tile)[None] * grazed


def solution(mesh):
    placed = (
        P("tracer", None, "gx", "gy"),
        P(None, "tracer", "gx", "gy"),
        P("gx", "gy"),
        P("gx", "gy"),
        P("gx", "gy"),
        P(None, "gx", "gy"),
        P("tracer"),
        P(),
    )
    return jax.shard_map(
        on_device,
        mesh=mesh,
        in_specs=placed,
        out_specs=P("tracer", None, "gx", "gy"),
        check_vma=False,
    )
```

```python
import functools

import jax
import jax.numpy as jnp
from jax import lax
from jax.experimental import pallas as pl
from jax.experimental.pallas import tpu as pltpu
from jax.sharding import PartitionSpec as P

STEPS = 2
MESH = pl.DeviceIdType.MESH
F32 = jnp.float32
LANES = 128
LO, IN, HI = 6, 8, 16


def minmod(a, b):
    return jnp.maximum(0.0, jnp.minimum(a, b)) + jnp.minimum(0.0, jnp.maximum(a, b))


def roll(v, shift):
    return pltpu.roll(v, shift % LANES, 1)


def kernel(
    dims, tr, fl, de, dn, dep, gz, grp, prf, adv, grazed, f2,
    ext, flv, dev, dnv, depv, gzv, grps, prfs, tv,
    cxs, cxl, cxh, cys, cyl, cyh, fa, fb, fx,
    pqs, pqr, rs, rr, f1, own1,
    sxl, sxh, xl, xh, yp, yl, yr, ge, yst, gsl, gsh, gxl, gxh, tx,
    hy, fy, ky, hz, fz, hx, kx, wx, ec,
    lsem, csem, crec, fas, far, fbs, fbr, pqss, pqrs, rss, rrs, f1s, f1r, f2s, f2r,
    xss, xrs, yss, yrs, gss, grs,
):
    nt, nx, ny, t_dev, lev, total = dims
    own = lev // nt
    me, gx, gy = lax.axis_index("tracer"), lax.axis_index("gx"), lax.axis_index("gy")
    left, right = lax.rem(gy + ny - 1, ny), lax.rem(gy + 1, ny)
    has_lo, has_hi = gx > 0, gx < nx - 1
    others = [lax.rem(me + d, nt) for d in range(1, nt)]

    loads = [
        (tr, ext.at[0, :, :, pl.ds(IN, 8), :]), (fl, flv), (de, dev), (dn, dnv), (dep, depv),
        (gz, gzv), (grp, grps), (prf, prfs),
    ]
    loads = [pltpu.make_async_copy(a, b, lsem.at[i]) for i, (a, b) in enumerate(loads)]

    barrier = pltpu.get_barrier_semaphore()
    for peer in others:
        pl.semaphore_signal(barrier, inc=1, device_id={"tracer": peer}, device_id_type=MESH)
    for z in (left, right):
        pl.semaphore_signal(barrier, inc=1, device_id={"gy": z}, device_id_type=MESH)

    @pl.when(has_lo)
    def _():
        pl.semaphore_signal(barrier, inc=1, device_id={"gx": gx - 1}, device_id_type=MESH)

    @pl.when(has_hi)
    def _():
        pl.semaphore_signal(barrier, inc=1, device_id={"gx": gx + 1}, device_id_type=MESH)

    for c in loads:
        c.start()

    lane = lax.broadcasted_iota(jnp.int32, (8, LANES), 1)
    row = lax.broadcasted_iota(jnp.int32, (8, LANES), 0)
    plev, e = lane // 8, lane % 8
    at_edge = (lane < 2) | (lane >= LANES - 2)
    zero = jnp.zeros((8, LANES), F32)

    def spread(v):
        base = jnp.where(lane < 8, roll(v, 4), zero)
        for s in (8, 16, 32, 64):
            base = base + roll(base, s)
        return base

    for c in loads[1:]:
        c.wait()
    for t in range(t_dev):
        w = jnp.full((8, LANES), prfs[grps[t]], F32)
        tv[t] = w
        tx[t // 4] = w if t % 4 == 0 else jnp.where(row // 2 == t % 4, w, tx[t // 4])
    depth = depv[...].astype(F32)
    cxs[0] = depth
    cxs[1] = dev[...]
    rows_tile = zero
    lanes_tile = zero
    for b in range(own):
        rows_tile = jnp.where(row == b, flv[0, b, pl.ds(7, 1), :], rows_tile)
        lanes_tile = jnp.where(plev == me * own + b, spread(flv[1, b]), lanes_tile)
    cxs[2] = rows_tile
    cys[0] = spread(depth)
    cys[1] = spread(dnv[...])
    cys[2] = lanes_tile
    for k in range(3):
        for b in range(own):
            fa[me, k * own + b] = flv[k, b]
    fa[me, 3 * own] = lanes_tile
    loads[0].wait()

    def send(src, dst, ssem, rsem, to):
        return pltpu.make_async_remote_copy(
            src_ref=src, dst_ref=dst, send_sem=ssem, recv_sem=rsem, device_id=to, device_id_type=MESH
        )

    def pack_level(s, l, tiles, acc):
        acc = list(acc)
        for t in range(t_dev):
            if s == 0:
                sxl[s, l, pl.ds(2 * t, 2), :] = ext[s, t, l, pl.ds(IN, 2), :]
                sxh[s, l, pl.ds(2 * t, 2), :] = ext[s, t, l, pl.ds(IN + 6, 2), :]
            acc[t] = jnp.where(plev == l, pltpu.roll(tiles[t], 8 * l + 4, 1), acc[t])
        return tuple(acc)

    def first(l, acc):
        tiles = [ext[0, t, l, pl.ds(IN, 8), :] for t in range(t_dev)]
        p_sum, q_sum = zero, zero
        for t in range(t_dev):
            w = tv[t]
            wc = w * tiles[t]
            p_sum = p_sum + wc
            q_sum = q_sum + w * wc
        j, b = l // own, lax.rem(l, own)
        pqs[j, b] = p_sum
        pqs[j, own + b] = q_sum
        return pack_level(0, l, tiles, acc)

    acc = lax.fori_loop(0, lev, first, tuple(zero for _ in range(t_dev)), unroll=4)
    for t in range(t_dev):
        yp[0, t] = acc[t]

    pl.semaphore_wait(barrier, nt - 1 + 2 + has_lo.astype(jnp.int32) + has_hi.astype(jnp.int32))

    c_right = send(cys, cyl, csem.at[0], crec.at[0], {"gy": right})
    c_left = send(cys.at[pl.ds(0, 1)], cyh, csem.at[1], crec.at[1], {"gy": left})
    c_up = send(cxs, cxl, csem.at[2], crec.at[2], {"gx": gx + 1})
    c_down = send(cxs.at[pl.ds(0, 1)], cxh, csem.at[3], crec.at[3], {"gx": gx - 1})
    c_right.start()
    c_left.start()
    pl.when(has_hi)(c_up.start)
    pl.when(has_lo)(c_down.start)

    def y_copies(s):
        return (
            send(yp.at[s], yl.at[s], yss.at[s, 0], yrs.at[s, 0], {"gy": right}),
            send(yp.at[s], yr.at[s], yss.at[s, 1], yrs.at[s, 1], {"gy": left}),
        )

    def x_copies(s, j):
        c = pl.ds(j * own, own)
        return (
            send(sxh.at[s, c], xl.at[s, c], xss.at[s, 0, j], xrs.at[s, 0, j], {"gx": gx + 1}),
            send(sxl.at[s, c], xh.at[s, c], xss.at[s, 1, j], xrs.at[s, 1, j], {"gx": gx - 1}),
        )

    def gather_start(buf, ssem, rsem):
        for d, peer in enumerate(others):
            send(buf.at[me], buf.at[me], ssem.at[d], rsem.at[me], {"tracer": peer}).start()

    def gather_wait(buf, ssem, rsem):
        for d, peer in enumerate(others):
            send(buf.at[me], buf.at[peer], ssem.at[d], rsem.at[peer], {"tracer": peer}).wait_recv()

    def gather_done(buf, ssem, rsem):
        for d, peer in enumerate(others):
            send(buf.at[me], buf.at[peer], ssem.at[d], rsem.at[peer], {"tracer": peer}).wait_send()

    def scatter(src, dst, ssem, rsem, peer):
        return send(src.at[peer], dst.at[me], ssem.at[peer], rsem.at[me], {"tracer": peer})

    def scatter_wait(src, dst, ssem, rsem):
        for peer in others:
            send(src.at[peer], dst.at[peer], ssem.at[peer], rsem.at[peer], {"tracer": peer}).wait_recv()

    for peer in others:
        scatter(pqs, pqr, pqss, pqrs, peer).start()
    gather_start(fa, fas, far)
    for c in y_copies(0):
        c.start()

    def x_start(s, j):
        up, down = x_copies(s, j)
        pl.when(has_hi)(up.start)
        pl.when(has_lo)(down.start)

    for j in range(nt):
        x_start(0, j)

    c_right.wait_recv()
    c_left.wait_recv()
    pl.when(has_hi)(c_down.wait_recv)

    @pl.when(has_lo)
    def _():
        c_up.wait_recv()

    @pl.when(gx == 0)
    def _():
        for k in range(3):
            cxl[k] = zero

    @pl.when(gx == nx - 1)
    def _():
        cxh[0] = zero

    fb[me, 0] = cxl[2]
    fb[me, 1] = cyl[2]
    gather_start(fb, fbs, fbr)

    dep_l = cyl[0] * (gy > 0).astype(F32)
    dep_r = cyh[0] * (gy < ny - 1).astype(F32)
    dep_m = cys[0]
    plevf = plev.astype(F32)
    wet0 = (plevf < jnp.where(e < 4, dep_l, dep_m)).astype(F32)
    wet1 = (plevf < jnp.where(e < 4, dep_m, dep_r)).astype(F32)
    open0 = wet0 * roll(wet0, 1)
    open1 = wet1 * roll(wet1, 1)
    wx[...] = jnp.zeros_like(wx)
    wx[pl.ds(LO, 2), :] = cxl[0, pl.ds(6, 2), :]
    wx[pl.ds(IN, 8), :] = depth
    wx[pl.ds(HI, 2), :] = cxh[0, pl.ds(0, 2), :]
    for k in range(2 * own):
        pqr[me, k] = pqs[me, k]
    scatter_wait(pqs, pqr, pqss, pqrs)
    scale = 4.0 / total
    for b in range(own):
        prey = pqr[0, b]
        sq = pqr[0, own + b]
        for j in range(1, nt):
            prey = prey + pqr[j, b]
            sq = sq + pqr[j, own + b]
        f1[me, b] = gzv[me * own + b] / (1.0 + scale * prey)
        own1[b] = sq
    gather_start(f1, f1s, f1r)

    gather_wait(fa, fas, far)
    flux_edge = fa[0, 3 * own]
    for j in range(1, nt):
        flux_edge = flux_edge + fa[j, 3 * own]
    ec[0] = 0.5 * open0
    ec[1] = flux_edge
    ec[2] = 2.0 * open0 * roll(jnp.where(e < 4, cyl[1], cys[1]), 1)
    ec[3] = 0.5 * open1
    ec[4] = roll(flux_edge, 1) * open1
    ec[5] = 2.0 * open1 * roll(cys[1], 1)
    dn_low = 2.0 * roll(dnv[...], 1)
    depth_y = jnp.minimum(depth, roll(depth, 1))

    for l in range(lev):
        j, b = l // own, l % own
        open_y = (depth_y > l).astype(F32)
        hy[l] = 0.5 * open_y
        fy[l] = roll(fa[j, own + b], 1) * open_y
        ky[l] = dn_low * open_y
        if l:
            open_z = (depth > l).astype(F32)
            hz[l] = 0.5 * open_z
            fz[l] = fa[(l - 1) // own, 2 * own + (l - 1) % own] * open_z
        fx[l, pl.ds(IN, 8), :] = fa[j, b]

    def edge(cells, h, flux, kappa):
        below = roll(cells, 1)
        jump = h * (cells - below)
        slope = minmod(jump, roll(jump, -1))
        carried = flux * jnp.where(flux > 0.0, below + roll(slope, 1), cells - slope) - kappa * jump
        return carried - roll(carried, -1)

    def y_edges(s):
        for c in y_copies(s):
            c.wait_recv()
        for t in range(t_dev):
            mine = yp[s, t]
            low = edge(jnp.where(e < 4, yl[s, t], mine), ec[0], ec[1], ec[2])
            high = edge(jnp.where(e < 4, mine, yr[s, t]), ec[3], ec[4], ec[5])
            ge[t] = jnp.where(e < 4, high, low)

    def z_part(s):
        def pair(p, carry):
            for h in range(2):
                t = 2 * p + h
                cells = [ext[s, t, l, pl.ds(IN, 8), :] for l in range(lev)]
                jumps = [zero] + [hz[l] * (cells[l] - cells[l - 1]) for l in range(1, lev)] + [zero]
                slopes = [minmod(jumps[l], jumps[l + 1]) for l in range(lev)]
                faces = [zero]
                for l in range(1, lev):
                    f = fz[l]
                    faces.append(f * jnp.where(f > 0.0, cells[l - 1] + slopes[l - 1], cells[l] - slopes[l]))
                faces.append(zero)
                for l in range(lev):
                    adv[t, l] = cells[l] + (faces[l] - faces[l + 1])
            return carry

        lax.fori_loop(0, t_dev // 2, pair, 0)

    group = 4
    steps = lev // group

    def y_part(s):
        def jumps(g):
            for i in range(group):
                h = hy[g * group + i]
                for t in range(t_dev):
                    c = ext[s, t, g * group + i, pl.ds(IN, 8), :]
                    yst[0, i, t] = h * (c - roll(c, 1))

        def slopes(g):
            for i in range(group):
                for t in range(t_dev):
                    c, jump = ext[s, t, g * group + i, pl.ds(IN, 8), :], yst[0, i, t]
                    slope = minmod(jump, roll(jump, -1))
                    yst[1, i, t] = c + slope
                    yst[2, i, t] = c - slope
                    yst[3, i, t] = jump

        def fluxes(g):
            for i in range(group):
                f, k = fy[g * group + i], ky[g * group + i]
                ahead = f > 0.0
                for t in range(t_dev):
                    face = jnp.where(ahead, roll(yst[1, i, t], 1), yst[2, i, t])
                    yst[4, i, t] = f * face - k * yst[3, i, t]

        def tendencies(g):
            for i in range(group):
                l = g * group + i
                for t in range(t_dev):
                    carried = yst[4, i, t]
                    outer = pltpu.roll(ge[t], (LANES - 4) - 8 * l, 1)
                    adv[t, l] = adv[t, l] + jnp.where(at_edge, outer, carried - roll(carried, -1))

        stages = (tendencies, fluxes, slopes, jumps)

        def step(g, carry):
            for k in range(4):
                stages[k](g - 3 + k)
            return carry

        for g in range(3):
            for m in range(g, -1, -1):
                stages[3 - m](g - m)
        lax.fori_loop(3, steps, step, 0)
        for g in range(steps, steps + 3):
            for m in range(3, g - steps, -1):
                stages[3 - m](g - m)

    def x_part(s):
        def chunk(j, carry):
            up, down = x_copies(s, j)
            pl.when(has_lo)(up.wait_recv)
            pl.when(has_hi)(down.wait_recv)
            for b in range(own):
                l = j * own + b
                if s:
                    for halo, fac in ((xl, gxl), (xh, gxh)):
                        two = pl.multiple_of(2 * l, 2)
                        f8 = jnp.where(row % 2 == 0, fac[pl.ds(two, 1), :], fac[pl.ds(two + 1, 1), :])
                        for k in range(2 * t_dev // 8):
                            r = pl.ds(8 * k, 8)
                            halo[1, l, r, :] = halo[1, l, r, :] - (tx[k] * f8) * halo[0, l, r, :]
                h = [hx[l, pl.ds(IN - 1 + k, 8), :] for k in range(4)]
                f = [fx[l, pl.ds(IN - 1 + k, 8), :] for k in range(2)]
                kk = [kx[l, pl.ds(IN + k, 8), :] for k in range(2)]
                ahead = [f[k] > 0.0 for k in range(2)]
                total_r = zero
                for t in range(t_dev):
                    two = pl.ds(2 * t, 2)
                    ext[s, t, l, pl.ds(LO, 2), :] = xl[s, l, two, :]
                    ext[s, t, l, pl.ds(HI, 2), :] = xh[s, l, two, :]
                    c = [ext[s, t, l, pl.ds(LO + k, 8), :] for k in range(5)]
                    jump = [h[k] * (c[k + 1] - c[k]) for k in range(4)]
                    slope = [minmod(jump[k], jump[k + 1]) for k in range(3)]
                    carried = [
                        f[k] * jnp.where(ahead[k], c[k + 1] + slope[k], c[k + 2] - slope[k + 1])
                        - kk[k] * jump[k + 1]
                        for k in range(2)
                    ]
                    a = adv[t, l] + (carried[0] - carried[1])
                    adv[t, l] = a
                    if s == 0:
                        total_r = total_r + tv[t] * a
                        sxl[1, l, two, :] = adv[t, l, pl.ds(0, 2), :]
                        sxh[1, l, two, :] = adv[t, l, pl.ds(6, 2), :]
                if s == 0:
                    rs[j, b] = total_r
            if s == 0:
                @pl.when(j != me)
                def _():
                    scatter(rs, rr, rss, rrs, j).start()

                x_start(1, j)
            return carry

        lax.fori_loop(0, nt, chunk, 0)

    for s in range(STEPS):
        @pl.when(gx == 0)
        def _():
            xl[s] = jnp.zeros_like(xl[s])

        @pl.when(gx == nx - 1)
        def _():
            xh[s] = jnp.zeros_like(xh[s])

    gather_wait(fb, fbs, fbr)
    flux_edge = fb[0, 1]
    for j in range(1, nt):
        flux_edge = flux_edge + fb[j, 1]
    ec[1] = roll(jnp.where(e < 4, flux_edge, ec[1]), 1) * open0
    for l in range(lev):
        fx[l, pl.ds(IN - 1, 1), :] = fb[l // own, 0, pl.ds(l % own, 1), :]
    d_low = jnp.concatenate([2.0 * cxl[1, pl.ds(7, 1), :], 2.0 * dev[pl.ds(0, 7), :]], axis=0)
    d_up = 2.0 * dev[...]
    depth_x = [
        jnp.minimum(wx[pl.ds(LO + k, 8), :], wx[pl.ds(LO + 1 + k, 8), :]) for k in range(4)
    ]
    for l in range(lev):
        opens = [(depth_x[k] > l).astype(F32) for k in range(4)]
        low = fx[l, pl.ds(IN - 1, 8), :] * opens[1]
        up = fx[l, pl.ds(IN, 8), :] * opens[2]
        hx[l, pl.ds(IN - 1, 8), :] = 0.5 * opens[0]
        hx[l, pl.ds(IN + 2, 8), :] = 0.5 * opens[3]
        fx[l, pl.ds(IN - 1, 8), :] = low
        fx[l, pl.ds(IN, 8), :] = up
        kx[l, pl.ds(IN, 8), :] = d_low * opens[1]
        kx[l, pl.ds(IN + 1, 8), :] = d_up * opens[2]

    z_part(0)
    y_edges(0)
    y_part(0)
    x_part(0)
    gather_wait(f1, f1s, f1r)
    for l in range(lev):
        gsl[pl.ds(2 * l, 2), :] = f1[l // own, l % own, pl.ds(0, 2), :]
        gsh[pl.ds(2 * l, 2), :] = f1[l // own, l % own, pl.ds(6, 2), :]
    g_up = send(gsh, gxl, gss.at[0], grs.at[0], {"gx": gx + 1})
    g_down = send(gsl, gxh, gss.at[1], grs.at[1], {"gx": gx - 1})
    pl.when(has_hi)(g_up.start)
    pl.when(has_lo)(g_down.start)

    def second(l, acc):
        j, b = l // own, lax.rem(l, own)
        factor = f1[j, b]
        tiles = []
        for t in range(t_dev):
            c = adv[t, l] - (tv[t] * factor) * ext[0, t, l, pl.ds(IN, 8), :]
            ext[1, t, l, pl.ds(IN, 8), :] = c
            grazed[t, l] = tv[t] * c
            tiles.append(c)
        return pack_level(1, l, tiles, acc)

    acc = lax.fori_loop(0, lev, second, tuple(zero for _ in range(t_dev)), unroll=4)
    for t in range(t_dev):
        yp[1, t] = acc[t]
    for c in y_copies(1):
        c.start()
    z_part(1)

    for b in range(own):
        rr[me, b] = rs[me, b]
    scatter_wait(rs, rr, rss, rrs)
    for b in range(own):
        prey = rr[0, b]
        for j in range(1, nt):
            prey = prey + rr[j, b]
        prey = prey - f1[me, b] * own1[b]
        f2[me, b] = gzv[me * own + b] / (1.0 + scale * prey)
    gather_start(f2, f2s, f2r)

    y_edges(1)
    y_part(1)
    pl.when(has_lo)(g_up.wait_recv)
    pl.when(has_hi)(g_down.wait_recv)

    @pl.when(gx == 0)
    def _():
        gxl[...] = jnp.zeros_like(gxl)

    @pl.when(gx == nx - 1)
    def _():
        gxh[...] = jnp.zeros_like(gxh)

    x_part(1)
    gather_wait(f2, f2s, f2r)

    c_right.wait_send()
    c_left.wait_send()
    pl.when(has_hi)(c_up.wait_send)
    pl.when(has_lo)(c_down.wait_send)
    pl.when(has_hi)(g_up.wait_send)
    pl.when(has_lo)(g_down.wait_send)
    for s in range(STEPS):
        for c in y_copies(s):
            c.wait_send()
        for j in range(nt):
            up, down = x_copies(s, j)
            pl.when(has_hi)(up.wait_send)
            pl.when(has_lo)(down.wait_send)
    gather_done(fa, fas, far)
    gather_done(fb, fbs, fbr)
    gather_done(f1, f1s, f1r)
    gather_done(f2, f2s, f2r)
    for peer in others:
        scatter(pqs, pqr, pqss, pqrs, peer).wait_send()
        scatter(rs, rr, rss, rrs, peer).wait_send()


def on_device(tracers, fluxes, diff_east, diff_north, column_depth, grazers, groups, preference):
    t_dev, lev, rows, cols = tracers.shape
    nt, nx, ny = (lax.axis_size(a) for a in ("tracer", "gx", "gy"))
    own = lev // nt
    tile = (8, LANES)
    dma = pltpu.SemaphoreType.DMA

    def v(*shape):
        return pltpu.VMEM(shape, F32)

    scratch = [
        v(2, t_dev, lev, 24, LANES),
        v(3, own, *tile), v(*tile), v(*tile), pltpu.VMEM(tile, jnp.int32), v(lev, *tile),
        pltpu.SMEM(groups.shape, jnp.int32), pltpu.SMEM(preference.shape, F32), v(t_dev, *tile),
        v(3, *tile), v(3, *tile), v(1, *tile), v(3, *tile), v(3, *tile), v(1, *tile),
        v(nt, 3 * own + 1, *tile), v(nt, 2, *tile), v(lev, 24, LANES),
        v(nt, 2 * own, *tile), v(nt, 2 * own, *tile), v(nt, own, *tile), v(nt, own, *tile),
        v(nt, own, *tile), v(own, *tile),
        v(2, lev, 2 * t_dev, LANES), v(2, lev, 2 * t_dev, LANES),
        v(2, lev, 2 * t_dev, LANES), v(2, lev, 2 * t_dev, LANES),
        v(2, t_dev, *tile), v(2, t_dev, *tile), v(2, t_dev, *tile), v(t_dev, *tile), v(5, 4, t_dev, *tile),
        v(2 * lev, LANES), v(2 * lev, LANES), v(2 * lev, LANES), v(2 * lev, LANES), v(2 * t_dev // 8, *tile),
        v(lev, *tile), v(lev, *tile), v(lev, *tile), v(lev, *tile), v(lev, *tile),
        v(lev, 24, LANES), v(lev, 24, LANES), v(24, LANES), v(6, *tile),
        dma((8,)), dma((4,)), dma((4,)),
        dma((nt,)), dma((nt,)), dma((nt,)), dma((nt,)), dma((nt,)), dma((nt,)),
        dma((nt,)), dma((nt,)), dma((nt,)), dma((nt,)), dma((nt,)), dma((nt,)),
        dma((2, 2, nt)), dma((2, 2, nt)), dma((2, 2)), dma((2, 2)), dma((2,)), dma((2,)),
    ]
    moved, grazed, factor = pl.pallas_call(
        functools.partial(kernel, (nt, nx, ny, t_dev, lev, t_dev * nt)),
        out_shape=(
            jax.ShapeDtypeStruct(tracers.shape, F32),
            jax.ShapeDtypeStruct(tracers.shape, F32),
            jax.ShapeDtypeStruct((nt, own, *tile), F32),
        ),
        in_specs=[pl.BlockSpec(memory_space=pltpu.HBM)] * 8,
        out_specs=[pl.BlockSpec(memory_space=pltpu.VMEM)] * 3,
        scratch_shapes=scratch,
        compiler_params=pltpu.CompilerParams(
            collective_id=0, has_side_effects=True, vmem_limit_bytes=20 * 1024 * 1024
        ),
        name="plankton",
    )(*[
        pltpu.with_memory_space_constraint(a, pltpu.HBM)
        for a in (tracers, fluxes, diff_east, diff_north, column_depth, grazers, groups, preference)
    ])
    return moved - factor.reshape(lev, *tile)[None] * grazed


def solution(mesh):
    placed = (
        P("tracer", None, "gx", "gy"),
        P(None, "tracer", "gx", "gy"),
        P("gx", "gy"),
        P("gx", "gy"),
        P("gx", "gy"),
        P(None, "gx", "gy"),
        P("tracer"),
        P(),
    )
    return jax.shard_map(
        on_device,
        mesh=mesh,
        in_specs=placed,
        out_specs=P("tracer", None, "gx", "gy"),
        check_vma=False,
    )
```

```python
import functools

import jax
import jax.numpy as jnp
from jax import lax
from jax.experimental import pallas as pl
from jax.experimental.pallas import tpu as pltpu
from jax.sharding import PartitionSpec as P

STEPS = 2
MESH = pl.DeviceIdType.MESH
F32 = jnp.float32
LANES = 128
LO, IN, HI = 6, 8, 16


def minmod(a, b):
    return jnp.maximum(0.0, jnp.minimum(a, b)) + jnp.minimum(0.0, jnp.maximum(a, b))


def roll(v, shift):
    return pltpu.roll(v, shift % LANES, 1)


def kernel(
    dims, tr, fl, de, dn, dep, gz, grp, prf, adv, grazed, f2,
    ext, dev, dnv, depv, gzv, grps, prfs, tv,
    cxs, cxl, cxh, cys, cyl, cyh, fa, fxs, fxl, fes, fel, fx,
    pqs, pqr, rs, rr, f1, own1,
    sxl, sxh, xl, xh, yp, yl, yr, ge, yst, gsl, gsh, gxl, gxh, tx,
    hy, fy, ky, hz, fz, hx, kx, wx, ec,
    lsem, csem, crec, fas, far, pqss, pqrs, rss, rrs, f1s, f1r, f2s, f2r,
    xss, xrs, yss, yrs, gss, grs,
):
    nt, nx, ny, t_dev, lev, total = dims
    own = lev // nt
    me, gx, gy = lax.axis_index("tracer"), lax.axis_index("gx"), lax.axis_index("gy")
    left, right = gy - 1, gy + 1
    has_left, has_right = gy > 0, gy < ny - 1
    has_lo, has_hi = gx > 0, gx < nx - 1
    others = [lax.rem(me + d, nt) for d in range(1, nt)]

    loads = [(fl, fa.at[me]), (de, dev), (dn, dnv), (dep, depv), (grp, grps), (prf, prfs), (gz, gzv)]
    for j in range(nt):
        c = pl.ds(j * own, own)
        loads.append((tr.at[:, c], ext.at[0, :, c, pl.ds(IN, 8), :]))
    loads = [pltpu.make_async_copy(a, b, lsem.at[i]) for i, (a, b) in enumerate(loads)]

    barrier = pltpu.get_barrier_semaphore()
    for peer in others:
        pl.semaphore_signal(barrier, inc=1, device_id={"tracer": peer}, device_id_type=MESH)

    @pl.when(has_left)
    def _():
        pl.semaphore_signal(barrier, inc=1, device_id={"gy": left}, device_id_type=MESH)

    @pl.when(has_right)
    def _():
        pl.semaphore_signal(barrier, inc=1, device_id={"gy": right}, device_id_type=MESH)

    @pl.when(has_lo)
    def _():
        pl.semaphore_signal(barrier, inc=1, device_id={"gx": gx - 1}, device_id_type=MESH)

    @pl.when(has_hi)
    def _():
        pl.semaphore_signal(barrier, inc=1, device_id={"gx": gx + 1}, device_id_type=MESH)

    for c in loads:
        c.start()

    lane = lax.broadcasted_iota(jnp.int32, (8, LANES), 1)
    row = lax.broadcasted_iota(jnp.int32, (8, LANES), 0)
    plev, e = lane // 8, lane % 8
    at_edge = (lane < 2) | (lane >= LANES - 2)
    zero = jnp.zeros((8, LANES), F32)

    def spread(v):
        base = jnp.where(lane < 8, roll(v, 4), zero)
        for s in (8, 16, 32, 64):
            base = base + roll(base, s)
        return base

    def send(src, dst, ssem, rsem, to):
        return pltpu.make_async_remote_copy(
            src_ref=src, dst_ref=dst, send_sem=ssem, recv_sem=rsem, device_id=to, device_id_type=MESH
        )

    fa_out = [
        send(fl, fa.at[me], fas.at[d], far.at[me], {"tracer": peer}) for d, peer in enumerate(others)
    ]

    near = [has_lo, has_hi, has_left, has_right]
    pl.semaphore_wait(barrier, nt - 1 + sum(h.astype(jnp.int32) for h in near))
    for c in fa_out:
        c.start()

    for c in loads[:6]:
        c.wait()
    for t in range(t_dev):
        w = jnp.full((8, LANES), prfs[grps[t]], F32)
        tv[t] = w
        tx[t // 4] = w if t % 4 == 0 else jnp.where(row // 2 == t % 4, w, tx[t // 4])
    depth = depv[...].astype(F32)
    cxs[0] = depth
    cxs[1] = dev[...]
    cys[0] = spread(depth)
    cys[1] = spread(dnv[...])
    c_right = send(cys, cyl, csem.at[0], crec.at[0], {"gy": right})
    c_left = send(cys.at[pl.ds(0, 1)], cyh, csem.at[1], crec.at[1], {"gy": left})
    c_up = send(cxs, cxl, csem.at[2], crec.at[2], {"gx": gx + 1})
    c_down = send(cxs.at[pl.ds(0, 1)], cxh, csem.at[3], crec.at[3], {"gx": gx - 1})
    pl.when(has_right)(c_right.start)
    pl.when(has_left)(c_left.start)
    pl.when(has_hi)(c_up.start)
    pl.when(has_lo)(c_down.start)

    def y_copies(s):
        return (
            send(yp.at[s], yl.at[s], yss.at[s, 0], yrs.at[s, 0], {"gy": right}),
            send(yp.at[s], yr.at[s], yss.at[s, 1], yrs.at[s, 1], {"gy": left}),
        )

    def y_start(s):
        to_right, to_left = y_copies(s)
        pl.when(has_right)(to_right.start)
        pl.when(has_left)(to_left.start)

    def x_copies(s, j):
        c = pl.ds(j * own, own)
        return (
            send(sxh.at[s, c], xl.at[s, c], xss.at[s, 0, j], xrs.at[s, 0, j], {"gx": gx + 1}),
            send(sxl.at[s, c], xh.at[s, c], xss.at[s, 1, j], xrs.at[s, 1, j], {"gx": gx - 1}),
        )

    def gather_start(buf, ssem, rsem):
        for d, peer in enumerate(others):
            send(buf.at[me], buf.at[me], ssem.at[d], rsem.at[me], {"tracer": peer}).start()

    def gather_wait(buf, ssem, rsem):
        for d, peer in enumerate(others):
            send(buf.at[me], buf.at[peer], ssem.at[d], rsem.at[peer], {"tracer": peer}).wait_recv()

    def gather_done(buf, ssem, rsem):
        for d, peer in enumerate(others):
            send(buf.at[me], buf.at[peer], ssem.at[d], rsem.at[peer], {"tracer": peer}).wait_send()

    def scatter(src, dst, ssem, rsem, peer):
        return send(src.at[peer], dst.at[me], ssem.at[peer], rsem.at[me], {"tracer": peer})

    def scatter_wait(src, dst, ssem, rsem):
        for peer in others:
            send(src.at[peer], dst.at[peer], ssem.at[peer], rsem.at[peer], {"tracer": peer}).wait_recv()

    def x_start(s, j):
        up, down = x_copies(s, j)
        pl.when(has_hi)(up.start)
        pl.when(has_lo)(down.start)

    for j in range(nt):
        loads[7 + j].wait()
        for b in range(own):
            l = j * own + b
            p_sum, q_sum = zero, zero
            for t in range(t_dev):
                two, tile = pl.ds(2 * t, 2), ext[0, t, l, pl.ds(IN, 8), :]
                sxl[0, l, two, :] = ext[0, t, l, pl.ds(IN, 2), :]
                sxh[0, l, two, :] = ext[0, t, l, pl.ds(IN + 6, 2), :]
                w = tv[t]
                wc = w * tile
                p_sum = p_sum + wc
                q_sum = q_sum + w * wc
            pqs[j, b] = p_sum
            pqs[j, own + b] = q_sum
        x_start(0, j)

        @pl.when(j != me)
        def _():
            scatter(pqs, pqr, pqss, pqrs, j).start()


    def pack_level(s, l, acc):
        tiles = [ext[s, t, l, pl.ds(IN, 8), :] for t in range(t_dev)]
        return tuple(
            jnp.where(plev == l, pltpu.roll(tiles[t], 8 * l + 4, 1), acc[t]) for t in range(t_dev)
        )

    blank = tuple(zero for _ in range(t_dev))
    acc = lax.fori_loop(0, lev, lambda l, acc: pack_level(0, l, acc), blank, unroll=4)
    for t in range(t_dev):
        yp[0, t] = acc[t]
    y_start(0)

    dn_low = 2.0 * roll(dnv[...], 1)
    depth_y = jnp.minimum(depth, roll(depth, 1))
    for l in range(lev):
        open_y = (depth_y > l).astype(F32)
        hy[l] = 0.5 * open_y
        ky[l] = dn_low * open_y
        if l:
            hz[l] = 0.5 * (depth > l).astype(F32)

    pl.when(has_left)(c_right.wait_recv)
    pl.when(has_right)(c_left.wait_recv)
    pl.when(has_hi)(c_down.wait_recv)

    @pl.when(has_lo)
    def _():
        c_up.wait_recv()

    @pl.when(gx == 0)
    def _():
        for k in range(2):
            cxl[k] = zero

    @pl.when(gx == nx - 1)
    def _():
        cxh[0] = zero

    @pl.when(gy == 0)
    def _():
        for k in range(2):
            cyl[k] = zero
        fel[...] = zero
        yl[...] = jnp.zeros_like(yl)

    @pl.when(gy == ny - 1)
    def _():
        cyh[0] = zero
        yr[...] = jnp.zeros_like(yr)

    dep_l, dep_r = cyl[0], cyh[0]
    dep_m = cys[0]
    plevf = plev.astype(F32)
    wet0 = (plevf < jnp.where(e < 4, dep_l, dep_m)).astype(F32)
    wet1 = (plevf < jnp.where(e < 4, dep_m, dep_r)).astype(F32)
    open0 = wet0 * roll(wet0, 1)
    open1 = wet1 * roll(wet1, 1)
    wx[...] = jnp.zeros_like(wx)
    wx[pl.ds(LO, 2), :] = cxl[0, pl.ds(6, 2), :]
    wx[pl.ds(IN, 8), :] = depth
    wx[pl.ds(HI, 2), :] = cxh[0, pl.ds(0, 2), :]
    d_low = jnp.concatenate([2.0 * cxl[1, pl.ds(7, 1), :], 2.0 * dev[pl.ds(0, 7), :]], axis=0)
    d_up = 2.0 * dev[...]
    depth_x = [
        jnp.minimum(wx[pl.ds(LO + k, 8), :], wx[pl.ds(LO + 1 + k, 8), :]) for k in range(4)
    ]
    for l in range(lev):
        opens = [(depth_x[k] > l).astype(F32) for k in range(4)]
        hx[l, pl.ds(IN - 1, 8), :] = 0.5 * opens[0]
        hx[l, pl.ds(IN + 2, 8), :] = 0.5 * opens[3]
        kx[l, pl.ds(IN, 8), :] = d_low * opens[1]
        kx[l, pl.ds(IN + 1, 8), :] = d_up * opens[2]
    for peer in others:
        send(fl, fa.at[peer], fas.at[0], far.at[peer], {"tracer": peer}).wait_recv()
    flux_edge = zero
    for l in range(lev):
        j, b = l // own, l % own
        flux_edge = jnp.where(plev == l, roll(fa[j, 1, b], 8 * l + 4), flux_edge)
        fxs[pl.ds(l, 1), :] = fa[j, 0, b, pl.ds(7, 1), :]
    fes[...] = flux_edge
    f_right = send(fes, fel, csem.at[4], crec.at[4], {"gy": right})
    f_up = send(fxs, fxl, csem.at[5], crec.at[5], {"gx": gx + 1})
    pl.when(has_right)(f_right.start)
    pl.when(has_hi)(f_up.start)
    ec[0] = 0.5 * open0
    ec[1] = flux_edge
    ec[2] = 2.0 * open0 * roll(jnp.where(e < 4, cyl[1], cys[1]), 1)
    ec[3] = 0.5 * open1
    ec[4] = roll(flux_edge, 1) * open1
    ec[5] = 2.0 * open1 * roll(cys[1], 1)
    for l in range(lev):
        j, b = l // own, l % own
        fy[l] = roll(fa[j, 1, b], 1) * (depth_y > l).astype(F32)
        if l:
            fz[l] = fa[(l - 1) // own, 2, (l - 1) % own] * (depth > l).astype(F32)
        fx[l, pl.ds(IN, 8), :] = fa[j, 0, b]

    def edge(cells, h, flux, kappa):
        below = roll(cells, 1)
        jump = h * (cells - below)
        slope = minmod(jump, roll(jump, -1))
        carried = flux * jnp.where(flux > 0.0, below + roll(slope, 1), cells - slope) - kappa * jump
        return carried - roll(carried, -1)

    def y_edges(s):
        from_left, from_right = y_copies(s)
        pl.when(has_left)(from_left.wait_recv)
        pl.when(has_right)(from_right.wait_recv)
        for t in range(t_dev):
            mine = yp[s, t]
            low = edge(jnp.where(e < 4, yl[s, t], mine), ec[0], ec[1], ec[2])
            high = edge(jnp.where(e < 4, mine, yr[s, t]), ec[3], ec[4], ec[5])
            ge[t] = jnp.where(e < 4, high, low)

    def z_part(s):
        def pair(p, carry):
            for h in range(2):
                t = 2 * p + h
                cells = [ext[s, t, l, pl.ds(IN, 8), :] for l in range(lev)]
                jumps = [zero] + [hz[l] * (cells[l] - cells[l - 1]) for l in range(1, lev)] + [zero]
                slopes = [minmod(jumps[l], jumps[l + 1]) for l in range(lev)]
                faces = [zero]
                for l in range(1, lev):
                    f = fz[l]
                    faces.append(f * jnp.where(f > 0.0, cells[l - 1] + slopes[l - 1], cells[l] - slopes[l]))
                faces.append(zero)
                for l in range(lev):
                    adv[t, l] = cells[l] + (faces[l] - faces[l + 1])
            return carry

        lax.fori_loop(0, t_dev // 2, pair, 0)

    group = 4
    steps = lev // group

    def y_part(s):
        def jumps(g):
            for i in range(group):
                h = hy[g * group + i]
                for t in range(t_dev):
                    c = ext[s, t, g * group + i, pl.ds(IN, 8), :]
                    yst[0, i, t] = h * (c - roll(c, 1))

        def slopes(g):
            for i in range(group):
                for t in range(t_dev):
                    c, jump = ext[s, t, g * group + i, pl.ds(IN, 8), :], yst[0, i, t]
                    slope = minmod(jump, roll(jump, -1))
                    yst[1, i, t] = c + slope
                    yst[2, i, t] = c - slope
                    yst[3, i, t] = jump

        def fluxes(g):
            for i in range(group):
                f, k = fy[g * group + i], ky[g * group + i]
                ahead = f > 0.0
                for t in range(t_dev):
                    face = jnp.where(ahead, roll(yst[1, i, t], 1), yst[2, i, t])
                    yst[4, i, t] = f * face - k * yst[3, i, t]

        def tendencies(g):
            for i in range(group):
                l = g * group + i
                for t in range(t_dev):
                    carried = yst[4, i, t]
                    outer = pltpu.roll(ge[t], (LANES - 4) - 8 * l, 1)
                    adv[t, l] = adv[t, l] + jnp.where(at_edge, outer, carried - roll(carried, -1))

        stages = (tendencies, fluxes, slopes, jumps)

        def step(g, carry):
            for k in range(4):
                stages[k](g - 3 + k)
            return carry

        for g in range(3):
            for m in range(g, -1, -1):
                stages[3 - m](g - m)
        lax.fori_loop(3, steps, step, 0)
        for g in range(steps, steps + 3):
            for m in range(3, g - steps, -1):
                stages[3 - m](g - m)

    def x_part(s):
        def chunk(j, carry):
            up, down = x_copies(s, j)
            pl.when(has_lo)(up.wait_recv)
            pl.when(has_hi)(down.wait_recv)
            for b in range(own):
                l = j * own + b
                if s:
                    for halo, fac in ((xl, gxl), (xh, gxh)):
                        two = pl.multiple_of(2 * l, 2)
                        f8 = jnp.where(row % 2 == 0, fac[pl.ds(two, 1), :], fac[pl.ds(two + 1, 1), :])
                        for k in range(2 * t_dev // 8):
                            r = pl.ds(8 * k, 8)
                            halo[1, l, r, :] = halo[1, l, r, :] - (tx[k] * f8) * halo[0, l, r, :]
                h = [hx[l, pl.ds(IN - 1 + k, 8), :] for k in range(4)]
                f = [fx[l, pl.ds(IN - 1 + k, 8), :] for k in range(2)]
                kk = [kx[l, pl.ds(IN + k, 8), :] for k in range(2)]
                ahead = [f[k] > 0.0 for k in range(2)]
                total_r = zero
                for t in range(t_dev):
                    two = pl.ds(2 * t, 2)
                    ext[s, t, l, pl.ds(LO, 2), :] = xl[s, l, two, :]
                    ext[s, t, l, pl.ds(HI, 2), :] = xh[s, l, two, :]
                    c = [ext[s, t, l, pl.ds(LO + k, 8), :] for k in range(5)]
                    jump = [h[k] * (c[k + 1] - c[k]) for k in range(4)]
                    slope = [minmod(jump[k], jump[k + 1]) for k in range(3)]
                    carried = [
                        f[k] * jnp.where(ahead[k], c[k + 1] + slope[k], c[k + 2] - slope[k + 1])
                        - kk[k] * jump[k + 1]
                        for k in range(2)
                    ]
                    a = adv[t, l] + (carried[0] - carried[1])
                    adv[t, l] = a
                    if s == 0:
                        total_r = total_r + tv[t] * a
                        sxl[1, l, two, :] = adv[t, l, pl.ds(0, 2), :]
                        sxh[1, l, two, :] = adv[t, l, pl.ds(6, 2), :]
                if s == 0:
                    rs[j, b] = total_r
            if s == 0:
                @pl.when(j != me)
                def _():
                    scatter(rs, rr, rss, rrs, j).start()

                x_start(1, j)
            return carry

        lax.fori_loop(0, nt, chunk, 0)

    for s in range(STEPS):
        @pl.when(gx == 0)
        def _():
            xl[s] = jnp.zeros_like(xl[s])

        @pl.when(gx == nx - 1)
        def _():
            xh[s] = jnp.zeros_like(xh[s])

    z_part(0)
    loads[6].wait()
    for k in range(2 * own):
        pqr[me, k] = pqs[me, k]
    scatter_wait(pqs, pqr, pqss, pqrs)
    scale = 4.0 / total
    for b in range(own):
        prey = pqr[0, b]
        sq = pqr[0, own + b]
        for j in range(1, nt):
            prey = prey + pqr[j, b]
            sq = sq + pqr[j, own + b]
        f1[me, b] = gzv[me * own + b] / (1.0 + scale * prey)
        own1[b] = sq
    gather_start(f1, f1s, f1r)

    pl.when(has_left)(f_right.wait_recv)
    ec[1] = roll(jnp.where(e < 4, fel[...], ec[1]), 1) * open0
    y_edges(0)
    y_part(0)
    pl.when(has_lo)(f_up.wait_recv)

    @pl.when(gx == 0)
    def _():
        fxl[...] = jnp.zeros_like(fxl)

    for l in range(lev):
        fx[l, pl.ds(IN - 1, 1), :] = fxl[pl.ds(l, 1), :]
    for l in range(lev):
        low = fx[l, pl.ds(IN - 1, 8), :] * (depth_x[1] > l).astype(F32)
        up = fx[l, pl.ds(IN, 8), :] * (depth_x[2] > l).astype(F32)
        fx[l, pl.ds(IN - 1, 8), :] = low
        fx[l, pl.ds(IN, 8), :] = up

    x_part(0)
    gather_wait(f1, f1s, f1r)
    for l in range(lev):
        gsl[pl.ds(2 * l, 2), :] = f1[l // own, l % own, pl.ds(0, 2), :]
        gsh[pl.ds(2 * l, 2), :] = f1[l // own, l % own, pl.ds(6, 2), :]
    g_up = send(gsh, gxl, gss.at[0], grs.at[0], {"gx": gx + 1})
    g_down = send(gsl, gxh, gss.at[1], grs.at[1], {"gx": gx - 1})
    pl.when(has_hi)(g_up.start)
    pl.when(has_lo)(g_down.start)

    def second(l, acc):
        acc = list(acc)
        j, b = l // own, lax.rem(l, own)
        factor = f1[j, b]
        for t in range(t_dev):
            c = adv[t, l] - (tv[t] * factor) * ext[0, t, l, pl.ds(IN, 8), :]
            ext[1, t, l, pl.ds(IN, 8), :] = c
            grazed[t, l] = tv[t] * c
            acc[t] = jnp.where(plev == l, pltpu.roll(c, 8 * l + 4, 1), acc[t])
        return tuple(acc)

    acc = lax.fori_loop(0, lev, second, blank, unroll=4)
    for t in range(t_dev):
        yp[1, t] = acc[t]
    y_start(1)
    z_part(1)

    for b in range(own):
        rr[me, b] = rs[me, b]
    scatter_wait(rs, rr, rss, rrs)
    for b in range(own):
        prey = rr[0, b]
        for j in range(1, nt):
            prey = prey + rr[j, b]
        prey = prey - f1[me, b] * own1[b]
        f2[me, b] = gzv[me * own + b] / (1.0 + scale * prey)
    gather_start(f2, f2s, f2r)

    y_edges(1)
    y_part(1)
    pl.when(has_lo)(g_up.wait_recv)
    pl.when(has_hi)(g_down.wait_recv)

    @pl.when(gx == 0)
    def _():
        gxl[...] = jnp.zeros_like(gxl)

    @pl.when(gx == nx - 1)
    def _():
        gxh[...] = jnp.zeros_like(gxh)

    x_part(1)
    gather_wait(f2, f2s, f2r)

    pl.when(has_right)(c_right.wait_send)
    pl.when(has_left)(c_left.wait_send)
    pl.when(has_hi)(c_up.wait_send)
    pl.when(has_lo)(c_down.wait_send)
    pl.when(has_hi)(g_up.wait_send)
    pl.when(has_lo)(g_down.wait_send)
    for s in range(STEPS):
        to_right, to_left = y_copies(s)
        pl.when(has_right)(to_right.wait_send)
        pl.when(has_left)(to_left.wait_send)
        for j in range(nt):
            up, down = x_copies(s, j)
            pl.when(has_hi)(up.wait_send)
            pl.when(has_lo)(down.wait_send)
    for c in fa_out:
        c.wait_send()
    pl.when(has_right)(f_right.wait_send)
    pl.when(has_hi)(f_up.wait_send)
    gather_done(f1, f1s, f1r)
    gather_done(f2, f2s, f2r)
    for peer in others:
        scatter(pqs, pqr, pqss, pqrs, peer).wait_send()
        scatter(rs, rr, rss, rrs, peer).wait_send()


def on_device(tracers, fluxes, diff_east, diff_north, column_depth, grazers, groups, preference):
    t_dev, lev, rows, cols = tracers.shape
    nt, nx, ny = (lax.axis_size(a) for a in ("tracer", "gx", "gy"))
    own = lev // nt
    tile = (8, LANES)
    dma = pltpu.SemaphoreType.DMA

    def v(*shape):
        return pltpu.VMEM(shape, F32)

    scratch = [
        v(2, t_dev, lev, 24, LANES),
        v(*tile), v(*tile), pltpu.VMEM(tile, jnp.int32), v(lev, *tile),
        pltpu.SMEM(groups.shape, jnp.int32), pltpu.SMEM(preference.shape, F32), v(t_dev, *tile),
        v(2, *tile), v(2, *tile), v(1, *tile), v(2, *tile), v(2, *tile), v(1, *tile),
        v(nt, 3, own, *tile), v(lev, LANES), v(lev, LANES), v(*tile), v(*tile), v(lev, 24, LANES),
        v(nt, 2 * own, *tile), v(nt, 2 * own, *tile), v(nt, own, *tile), v(nt, own, *tile),
        v(nt, own, *tile), v(own, *tile),
        v(2, lev, 2 * t_dev, LANES), v(2, lev, 2 * t_dev, LANES),
        v(2, lev, 2 * t_dev, LANES), v(2, lev, 2 * t_dev, LANES),
        v(2, t_dev, *tile), v(2, t_dev, *tile), v(2, t_dev, *tile), v(t_dev, *tile), v(5, 4, t_dev, *tile),
        v(2 * lev, LANES), v(2 * lev, LANES), v(2 * lev, LANES), v(2 * lev, LANES), v(2 * t_dev // 8, *tile),
        v(lev, *tile), v(lev, *tile), v(lev, *tile), v(lev, *tile), v(lev, *tile),
        v(lev, 24, LANES), v(lev, 24, LANES), v(24, LANES), v(6, *tile),
        dma((7 + nt,)), dma((6,)), dma((6,)),
        dma((nt,)), dma((nt,)), dma((nt,)), dma((nt,)),
        dma((nt,)), dma((nt,)), dma((nt,)), dma((nt,)), dma((nt,)), dma((nt,)),
        dma((2, 2, nt)), dma((2, 2, nt)), dma((2, 2)), dma((2, 2)), dma((2,)), dma((2,)),
    ]
    moved, grazed, factor = pl.pallas_call(
        functools.partial(kernel, (nt, nx, ny, t_dev, lev, t_dev * nt)),
        out_shape=(
            jax.ShapeDtypeStruct(tracers.shape, F32),
            jax.ShapeDtypeStruct(tracers.shape, F32),
            jax.ShapeDtypeStruct((nt, own, *tile), F32),
        ),
        in_specs=[pl.BlockSpec(memory_space=pltpu.HBM)] * 8,
        out_specs=[pl.BlockSpec(memory_space=pltpu.VMEM)] * 3,
        scratch_shapes=scratch,
        compiler_params=pltpu.CompilerParams(
            collective_id=0, has_side_effects=True, vmem_limit_bytes=20 * 1024 * 1024
        ),
        name="plankton",
    )(*[
        pltpu.with_memory_space_constraint(a, pltpu.HBM)
        for a in (tracers, fluxes, diff_east, diff_north, column_depth, grazers, groups, preference)
    ])
    return moved - factor.reshape(lev, *tile)[None] * grazed


def solution(mesh):
    placed = (
        P("tracer", None, "gx", "gy"),
        P(None, "tracer", "gx", "gy"),
        P("gx", "gy"),
        P("gx", "gy"),
        P("gx", "gy"),
        P(None, "gx", "gy"),
        P("tracer"),
        P(),
    )
    return jax.shard_map(
        on_device,
        mesh=mesh,
        in_specs=placed,
        out_specs=P("tracer", None, "gx", "gy"),
        check_vma=False,
    )
```

```python
import functools

import jax
import jax.numpy as jnp
from jax import lax
from jax.experimental import pallas as pl
from jax.experimental.pallas import tpu as pltpu
from jax.sharding import PartitionSpec as P

STEPS = 2
MESH = pl.DeviceIdType.MESH
F32 = jnp.float32
LANES = 128
LO, IN, HI = 6, 8, 16


def minmod(a, b):
    return jnp.maximum(0.0, jnp.minimum(a, b)) + jnp.minimum(0.0, jnp.maximum(a, b))


def roll(v, shift):
    return pltpu.roll(v, shift % LANES, 1)


def kernel(
    dims, tr, fl, de, dn, dep, gz, grp, prf, adv, grazed, f2,
    ext, dev, dnv, depv, gzv, grps, prfs, tv,
    cxs, cxl, cxh, cys, cyl, cyh, fa, fxs, fxl, fes, fel, fx,
    pqs, pqr, rs, rr, f1, own1,
    sxl, sxh, xl, xh, yp, yl, yr, ge, yst, gsl, gsh, gxl, gxh, tx,
    hy, fy, ky, hz, fz, hx, kx, wx, ec,
    lsem, csem, crec, fas, far, pqss, pqrs, rss, rrs, f1s, f1r, f2s, f2r,
    xss, xrs, yss, yrs, gss, grs,
):
    nt, nx, ny, t_dev, lev, total = dims
    own = lev // nt
    me, gx, gy = lax.axis_index("tracer"), lax.axis_index("gx"), lax.axis_index("gy")
    left, right = gy - 1, gy + 1
    has_left, has_right = gy > 0, gy < ny - 1
    has_lo, has_hi = gx > 0, gx < nx - 1
    others = [lax.rem(me + d, nt) for d in range(1, nt)]

    loads = [(fl, fa.at[me]), (de, dev), (dn, dnv), (dep, depv), (grp, grps), (prf, prfs), (gz, gzv)]
    for j in range(nt):
        c = pl.ds(j * own, own)
        loads.append((tr.at[:, c], ext.at[0, :, c, pl.ds(IN, 8), :]))
    loads = [pltpu.make_async_copy(a, b, lsem.at[i]) for i, (a, b) in enumerate(loads)]

    barrier = pltpu.get_barrier_semaphore()
    for peer in others:
        pl.semaphore_signal(barrier, inc=1, device_id={"tracer": peer}, device_id_type=MESH)

    @pl.when(has_left)
    def _():
        pl.semaphore_signal(barrier, inc=1, device_id={"gy": left}, device_id_type=MESH)

    @pl.when(has_right)
    def _():
        pl.semaphore_signal(barrier, inc=1, device_id={"gy": right}, device_id_type=MESH)

    @pl.when(has_lo)
    def _():
        pl.semaphore_signal(barrier, inc=1, device_id={"gx": gx - 1}, device_id_type=MESH)

    @pl.when(has_hi)
    def _():
        pl.semaphore_signal(barrier, inc=1, device_id={"gx": gx + 1}, device_id_type=MESH)

    for c in loads:
        c.start()

    lane = lax.broadcasted_iota(jnp.int32, (8, LANES), 1)
    row = lax.broadcasted_iota(jnp.int32, (8, LANES), 0)
    plev, e = lane // 8, lane % 8
    at_edge = (lane < 2) | (lane >= LANES - 2)
    zero = jnp.zeros((8, LANES), F32)

    def spread(v):
        base = jnp.where(lane < 8, roll(v, 4), zero)
        for s in (8, 16, 32, 64):
            base = base + roll(base, s)
        return base

    def send(src, dst, ssem, rsem, to):
        return pltpu.make_async_remote_copy(
            src_ref=src, dst_ref=dst, send_sem=ssem, recv_sem=rsem, device_id=to, device_id_type=MESH
        )

    fa_out = [
        send(fl, fa.at[me], fas.at[d], far.at[me], {"tracer": peer}) for d, peer in enumerate(others)
    ]

    near = [has_lo, has_hi, has_left, has_right]
    pl.semaphore_wait(barrier, nt - 1 + sum(h.astype(jnp.int32) for h in near))
    for c in fa_out:
        c.start()

    for c in loads[:6]:
        c.wait()
    for t in range(t_dev):
        w = jnp.full((8, LANES), prfs[grps[t]], F32)
        tv[t] = w
        tx[t // 4] = w if t % 4 == 0 else jnp.where(row // 2 == t % 4, w, tx[t // 4])
    depth = depv[...].astype(F32)
    cxs[0] = depth
    cxs[1] = dev[...]
    cys[0] = spread(depth)
    cys[1] = spread(dnv[...])
    c_right = send(cys, cyl, csem.at[0], crec.at[0], {"gy": right})
    c_left = send(cys.at[pl.ds(0, 1)], cyh, csem.at[1], crec.at[1], {"gy": left})
    c_up = send(cxs, cxl, csem.at[2], crec.at[2], {"gx": gx + 1})
    c_down = send(cxs.at[pl.ds(0, 1)], cxh, csem.at[3], crec.at[3], {"gx": gx - 1})
    pl.when(has_right)(c_right.start)
    pl.when(has_left)(c_left.start)
    pl.when(has_hi)(c_up.start)
    pl.when(has_lo)(c_down.start)

    def y_copies(s):
        return (
            send(yp.at[s], yl.at[s], yss.at[s, 0], yrs.at[s, 0], {"gy": right}),
            send(yp.at[s], yr.at[s], yss.at[s, 1], yrs.at[s, 1], {"gy": left}),
        )

    def y_start(s):
        to_right, to_left = y_copies(s)
        pl.when(has_right)(to_right.start)
        pl.when(has_left)(to_left.start)

    def x_copies(s, j):
        c = pl.ds(j * own, own)
        return (
            send(sxh.at[s, c], xl.at[s, c], xss.at[s, 0, j], xrs.at[s, 0, j], {"gx": gx + 1}),
            send(sxl.at[s, c], xh.at[s, c], xss.at[s, 1, j], xrs.at[s, 1, j], {"gx": gx - 1}),
        )

    def gather_start(buf, ssem, rsem):
        for d, peer in enumerate(others):
            send(buf.at[me], buf.at[me], ssem.at[d], rsem.at[me], {"tracer": peer}).start()

    def gather_wait(buf, ssem, rsem):
        for d, peer in enumerate(others):
            send(buf.at[me], buf.at[peer], ssem.at[d], rsem.at[peer], {"tracer": peer}).wait_recv()

    def gather_done(buf, ssem, rsem):
        for d, peer in enumerate(others):
            send(buf.at[me], buf.at[peer], ssem.at[d], rsem.at[peer], {"tracer": peer}).wait_send()

    def scatter(src, dst, ssem, rsem, peer):
        return send(src.at[peer], dst.at[me], ssem.at[peer], rsem.at[me], {"tracer": peer})

    def scatter_wait(src, dst, ssem, rsem):
        for peer in others:
            send(src.at[peer], dst.at[peer], ssem.at[peer], rsem.at[peer], {"tracer": peer}).wait_recv()

    def x_start(s, j):
        up, down = x_copies(s, j)
        pl.when(has_hi)(up.start)
        pl.when(has_lo)(down.start)

    for j in range(nt):
        loads[7 + j].wait()
        for b in range(own):
            l = j * own + b
            p_sum, q_sum = zero, zero
            for t in range(t_dev):
                two, tile = pl.ds(2 * t, 2), ext[0, t, l, pl.ds(IN, 8), :]
                sxl[0, l, two, :] = ext[0, t, l, pl.ds(IN, 2), :]
                sxh[0, l, two, :] = ext[0, t, l, pl.ds(IN + 6, 2), :]
                w = tv[t]
                wc = w * tile
                p_sum = p_sum + wc
                q_sum = q_sum + w * wc
            pqs[j, b] = p_sum
            pqs[j, own + b] = q_sum
        x_start(0, j)

        @pl.when(j != me)
        def _():
            scatter(pqs, pqr, pqss, pqrs, j).start()


    def pack_level(s, l, acc):
        tiles = [ext[s, t, l, pl.ds(IN, 8), :] for t in range(t_dev)]
        return tuple(
            jnp.where(plev == l, pltpu.roll(tiles[t], 8 * l + 4, 1), acc[t]) for t in range(t_dev)
        )

    blank = tuple(zero for _ in range(t_dev))
    acc = lax.fori_loop(0, lev, lambda l, acc: pack_level(0, l, acc), blank, unroll=4)
    for t in range(t_dev):
        yp[0, t] = acc[t]
    y_start(0)

    dn_low = 2.0 * roll(dnv[...], 1)
    depth_y = jnp.minimum(depth, roll(depth, 1))
    for l in range(lev):
        open_y = (depth_y > l).astype(F32)
        hy[l] = 0.5 * open_y
        ky[l] = dn_low * open_y
        if l:
            hz[l] = 0.5 * (depth > l).astype(F32)

    pl.when(has_left)(c_right.wait_recv)
    pl.when(has_right)(c_left.wait_recv)
    pl.when(has_hi)(c_down.wait_recv)

    @pl.when(has_lo)
    def _():
        c_up.wait_recv()

    @pl.when(gx == 0)
    def _():
        for k in range(2):
            cxl[k] = zero

    @pl.when(gx == nx - 1)
    def _():
        cxh[0] = zero

    @pl.when(gy == 0)
    def _():
        for k in range(2):
            cyl[k] = zero
        fel[...] = zero
        yl[...] = jnp.zeros_like(yl)

    @pl.when(gy == ny - 1)
    def _():
        cyh[0] = zero
        yr[...] = jnp.zeros_like(yr)

    dep_l, dep_r = cyl[0], cyh[0]
    dep_m = cys[0]
    plevf = plev.astype(F32)
    wet0 = (plevf < jnp.where(e < 4, dep_l, dep_m)).astype(F32)
    wet1 = (plevf < jnp.where(e < 4, dep_m, dep_r)).astype(F32)
    open0 = wet0 * roll(wet0, 1)
    open1 = wet1 * roll(wet1, 1)
    wx[...] = jnp.zeros_like(wx)
    wx[pl.ds(LO, 2), :] = cxl[0, pl.ds(6, 2), :]
    wx[pl.ds(IN, 8), :] = depth
    wx[pl.ds(HI, 2), :] = cxh[0, pl.ds(0, 2), :]
    d_low = jnp.concatenate([2.0 * cxl[1, pl.ds(7, 1), :], 2.0 * dev[pl.ds(0, 7), :]], axis=0)
    d_up = 2.0 * dev[...]
    depth_x = [
        jnp.minimum(wx[pl.ds(LO + k, 8), :], wx[pl.ds(LO + 1 + k, 8), :]) for k in range(4)
    ]
    for l in range(lev):
        opens = [(depth_x[k] > l).astype(F32) for k in range(4)]
        hx[l, pl.ds(IN - 1, 8), :] = 0.5 * opens[0]
        hx[l, pl.ds(IN + 2, 8), :] = 0.5 * opens[3]
        kx[l, pl.ds(IN, 8), :] = d_low * opens[1]
        kx[l, pl.ds(IN + 1, 8), :] = d_up * opens[2]
    for peer in others:
        send(fl, fa.at[peer], fas.at[0], far.at[peer], {"tracer": peer}).wait_recv()
    flux_edge = zero
    for l in range(lev):
        j, b = l // own, l % own
        flux_edge = jnp.where(plev == l, roll(fa[j, 1, b], 8 * l + 4), flux_edge)
        fxs[pl.ds(l, 1), :] = fa[j, 0, b, pl.ds(7, 1), :]
    fes[...] = flux_edge
    f_right = send(fes, fel, csem.at[4], crec.at[4], {"gy": right})
    f_up = send(fxs, fxl, csem.at[5], crec.at[5], {"gx": gx + 1})
    pl.when(has_right)(f_right.start)
    pl.when(has_hi)(f_up.start)

    loads[6].wait()
    for k in range(2 * own):
        pqr[me, k] = pqs[me, k]
    scatter_wait(pqs, pqr, pqss, pqrs)
    scale = 4.0 / total
    for b in range(own):
        prey = pqr[0, b]
        sq = pqr[0, own + b]
        for j in range(1, nt):
            prey = prey + pqr[j, b]
            sq = sq + pqr[j, own + b]
        f1[me, b] = gzv[me * own + b] / (1.0 + scale * prey)
        own1[b] = sq
    gather_start(f1, f1s, f1r)

    ec[0] = 0.5 * open0
    ec[1] = flux_edge
    ec[2] = 2.0 * open0 * roll(jnp.where(e < 4, cyl[1], cys[1]), 1)
    ec[3] = 0.5 * open1
    ec[4] = roll(flux_edge, 1) * open1
    ec[5] = 2.0 * open1 * roll(cys[1], 1)
    for l in range(lev):
        j, b = l // own, l % own
        fy[l] = roll(fa[j, 1, b], 1) * (depth_y > l).astype(F32)
        if l:
            fz[l] = fa[(l - 1) // own, 2, (l - 1) % own] * (depth > l).astype(F32)
        fx[l, pl.ds(IN, 8), :] = fa[j, 0, b]

    def edge(cells, h, flux, kappa):
        below = roll(cells, 1)
        jump = h * (cells - below)
        slope = minmod(jump, roll(jump, -1))
        carried = flux * jnp.where(flux > 0.0, below + roll(slope, 1), cells - slope) - kappa * jump
        return carried - roll(carried, -1)

    def y_edges(s):
        from_left, from_right = y_copies(s)
        pl.when(has_left)(from_left.wait_recv)
        pl.when(has_right)(from_right.wait_recv)
        for t in range(t_dev):
            mine = yp[s, t]
            low = edge(jnp.where(e < 4, yl[s, t], mine), ec[0], ec[1], ec[2])
            high = edge(jnp.where(e < 4, mine, yr[s, t]), ec[3], ec[4], ec[5])
            ge[t] = jnp.where(e < 4, high, low)

    def z_part(s):
        def pair(p, carry):
            for h in range(2):
                t = 2 * p + h
                cells = [ext[s, t, l, pl.ds(IN, 8), :] for l in range(lev)]
                jumps = [zero] + [hz[l] * (cells[l] - cells[l - 1]) for l in range(1, lev)] + [zero]
                slopes = [minmod(jumps[l], jumps[l + 1]) for l in range(lev)]
                faces = [zero]
                for l in range(1, lev):
                    f = fz[l]
                    faces.append(f * jnp.where(f > 0.0, cells[l - 1] + slopes[l - 1], cells[l] - slopes[l]))
                faces.append(zero)
                for l in range(lev):
                    adv[t, l] = cells[l] + (faces[l] - faces[l + 1])
            return carry

        lax.fori_loop(0, t_dev // 2, pair, 0)

    group = 4
    steps = lev // group

    def y_part(s):
        def jumps(g):
            for i in range(group):
                h = hy[g * group + i]
                for t in range(t_dev):
                    c = ext[s, t, g * group + i, pl.ds(IN, 8), :]
                    yst[0, i, t] = h * (c - roll(c, 1))

        def slopes(g):
            for i in range(group):
                for t in range(t_dev):
                    c, jump = ext[s, t, g * group + i, pl.ds(IN, 8), :], yst[0, i, t]
                    slope = minmod(jump, roll(jump, -1))
                    yst[1, i, t] = c + slope
                    yst[2, i, t] = c - slope
                    yst[3, i, t] = jump

        def fluxes(g):
            for i in range(group):
                f, k = fy[g * group + i], ky[g * group + i]
                ahead = f > 0.0
                for t in range(t_dev):
                    face = jnp.where(ahead, roll(yst[1, i, t], 1), yst[2, i, t])
                    yst[4, i, t] = f * face - k * yst[3, i, t]

        def tendencies(g):
            for i in range(group):
                l = g * group + i
                for t in range(t_dev):
                    carried = yst[4, i, t]
                    outer = zero if s else pltpu.roll(ge[t], (LANES - 4) - 8 * l, 1)
                    adv[t, l] = adv[t, l] + jnp.where(at_edge, outer, carried - roll(carried, -1))

        stages = (tendencies, fluxes, slopes, jumps)

        def step(g, carry):
            for k in range(4):
                stages[k](g - 3 + k)
            return carry

        for g in range(3):
            for m in range(g, -1, -1):
                stages[3 - m](g - m)
        lax.fori_loop(3, steps, step, 0)
        for g in range(steps, steps + 3):
            for m in range(3, g - steps, -1):
                stages[3 - m](g - m)

    def y_outer(l, carry):
        for t in range(t_dev):
            outer = pltpu.roll(ge[t], (LANES - 4) - 8 * l, 1)
            adv[t, l] = adv[t, l] + jnp.where(at_edge, outer, zero)
        return carry

    def x_part(s):
        def chunk(j, carry):
            up, down = x_copies(s, j)
            pl.when(has_lo)(up.wait_recv)
            pl.when(has_hi)(down.wait_recv)
            for b in range(own):
                l = j * own + b
                if s:
                    for halo, fac in ((xl, gxl), (xh, gxh)):
                        two = pl.multiple_of(2 * l, 2)
                        f8 = jnp.where(row % 2 == 0, fac[pl.ds(two, 1), :], fac[pl.ds(two + 1, 1), :])
                        for k in range(2 * t_dev // 8):
                            r = pl.ds(8 * k, 8)
                            halo[1, l, r, :] = halo[1, l, r, :] - (tx[k] * f8) * halo[0, l, r, :]
                h = [hx[l, pl.ds(IN - 1 + k, 8), :] for k in range(4)]
                f = [fx[l, pl.ds(IN - 1 + k, 8), :] for k in range(2)]
                kk = [kx[l, pl.ds(IN + k, 8), :] for k in range(2)]
                ahead = [f[k] > 0.0 for k in range(2)]
                total_r = zero
                for t in range(t_dev):
                    two = pl.ds(2 * t, 2)
                    ext[s, t, l, pl.ds(LO, 2), :] = xl[s, l, two, :]
                    ext[s, t, l, pl.ds(HI, 2), :] = xh[s, l, two, :]
                    c = [ext[s, t, l, pl.ds(LO + k, 8), :] for k in range(5)]
                    jump = [h[k] * (c[k + 1] - c[k]) for k in range(4)]
                    slope = [minmod(jump[k], jump[k + 1]) for k in range(3)]
                    carried = [
                        f[k] * jnp.where(ahead[k], c[k + 1] + slope[k], c[k + 2] - slope[k + 1])
                        - kk[k] * jump[k + 1]
                        for k in range(2)
                    ]
                    a = adv[t, l] + (carried[0] - carried[1])
                    adv[t, l] = a
                    if s == 0:
                        total_r = total_r + tv[t] * a
                        sxl[1, l, two, :] = adv[t, l, pl.ds(0, 2), :]
                        sxh[1, l, two, :] = adv[t, l, pl.ds(6, 2), :]
                if s == 0:
                    rs[j, b] = total_r
            if s == 0:
                @pl.when(j != me)
                def _():
                    scatter(rs, rr, rss, rrs, j).start()

                x_start(1, j)
            return carry

        lax.fori_loop(0, nt, chunk, 0)

    for s in range(STEPS):
        @pl.when(gx == 0)
        def _():
            xl[s] = jnp.zeros_like(xl[s])

        @pl.when(gx == nx - 1)
        def _():
            xh[s] = jnp.zeros_like(xh[s])

    z_part(0)
    pl.when(has_left)(f_right.wait_recv)
    ec[1] = roll(jnp.where(e < 4, fel[...], ec[1]), 1) * open0
    y_edges(0)
    y_part(0)
    pl.when(has_lo)(f_up.wait_recv)

    @pl.when(gx == 0)
    def _():
        fxl[...] = jnp.zeros_like(fxl)

    for l in range(lev):
        fx[l, pl.ds(IN - 1, 1), :] = fxl[pl.ds(l, 1), :]
    for l in range(lev):
        low = fx[l, pl.ds(IN - 1, 8), :] * (depth_x[1] > l).astype(F32)
        up = fx[l, pl.ds(IN, 8), :] * (depth_x[2] > l).astype(F32)
        fx[l, pl.ds(IN - 1, 8), :] = low
        fx[l, pl.ds(IN, 8), :] = up

    x_part(0)
    gather_wait(f1, f1s, f1r)
    for l in range(lev):
        gsl[pl.ds(2 * l, 2), :] = f1[l // own, l % own, pl.ds(0, 2), :]
        gsh[pl.ds(2 * l, 2), :] = f1[l // own, l % own, pl.ds(6, 2), :]
    g_up = send(gsh, gxl, gss.at[0], grs.at[0], {"gx": gx + 1})
    g_down = send(gsl, gxh, gss.at[1], grs.at[1], {"gx": gx - 1})
    pl.when(has_hi)(g_up.start)
    pl.when(has_lo)(g_down.start)

    def second(l, acc):
        acc = list(acc)
        j, b = l // own, lax.rem(l, own)
        factor = f1[j, b]
        for t in range(t_dev):
            c = adv[t, l] - (tv[t] * factor) * ext[0, t, l, pl.ds(IN, 8), :]
            ext[1, t, l, pl.ds(IN, 8), :] = c
            grazed[t, l] = tv[t] * c
            acc[t] = jnp.where(plev == l, pltpu.roll(c, 8 * l + 4, 1), acc[t])
        return tuple(acc)

    acc = lax.fori_loop(0, lev, second, blank, unroll=4)
    for t in range(t_dev):
        yp[1, t] = acc[t]
    y_start(1)
    z_part(1)
    y_part(1)

    for b in range(own):
        rr[me, b] = rs[me, b]
    scatter_wait(rs, rr, rss, rrs)
    for b in range(own):
        prey = rr[0, b]
        for j in range(1, nt):
            prey = prey + rr[j, b]
        prey = prey - f1[me, b] * own1[b]
        f2[me, b] = gzv[me * own + b] / (1.0 + scale * prey)
    gather_start(f2, f2s, f2r)

    pl.when(has_lo)(g_up.wait_recv)
    pl.when(has_hi)(g_down.wait_recv)

    @pl.when(gx == 0)
    def _():
        gxl[...] = jnp.zeros_like(gxl)

    @pl.when(gx == nx - 1)
    def _():
        gxh[...] = jnp.zeros_like(gxh)

    x_part(1)
    y_edges(1)
    lax.fori_loop(0, lev, y_outer, 0, unroll=4)
    gather_wait(f2, f2s, f2r)

    pl.when(has_right)(c_right.wait_send)
    pl.when(has_left)(c_left.wait_send)
    pl.when(has_hi)(c_up.wait_send)
    pl.when(has_lo)(c_down.wait_send)
    pl.when(has_hi)(g_up.wait_send)
    pl.when(has_lo)(g_down.wait_send)
    for s in range(STEPS):
        to_right, to_left = y_copies(s)
        pl.when(has_right)(to_right.wait_send)
        pl.when(has_left)(to_left.wait_send)
        for j in range(nt):
            up, down = x_copies(s, j)
            pl.when(has_hi)(up.wait_send)
            pl.when(has_lo)(down.wait_send)
    for c in fa_out:
        c.wait_send()
    pl.when(has_right)(f_right.wait_send)
    pl.when(has_hi)(f_up.wait_send)
    gather_done(f1, f1s, f1r)
    gather_done(f2, f2s, f2r)
    for peer in others:
        scatter(pqs, pqr, pqss, pqrs, peer).wait_send()
        scatter(rs, rr, rss, rrs, peer).wait_send()


def on_device(tracers, fluxes, diff_east, diff_north, column_depth, grazers, groups, preference):
    t_dev, lev, rows, cols = tracers.shape
    nt, nx, ny = (lax.axis_size(a) for a in ("tracer", "gx", "gy"))
    own = lev // nt
    tile = (8, LANES)
    dma = pltpu.SemaphoreType.DMA

    def v(*shape):
        return pltpu.VMEM(shape, F32)

    scratch = [
        v(2, t_dev, lev, 24, LANES),
        v(*tile), v(*tile), pltpu.VMEM(tile, jnp.int32), v(lev, *tile),
        pltpu.SMEM(groups.shape, jnp.int32), pltpu.SMEM(preference.shape, F32), v(t_dev, *tile),
        v(2, *tile), v(2, *tile), v(1, *tile), v(2, *tile), v(2, *tile), v(1, *tile),
        v(nt, 3, own, *tile), v(lev, LANES), v(lev, LANES), v(*tile), v(*tile), v(lev, 24, LANES),
        v(nt, 2 * own, *tile), v(nt, 2 * own, *tile), v(nt, own, *tile), v(nt, own, *tile),
        v(nt, own, *tile), v(own, *tile),
        v(2, lev, 2 * t_dev, LANES), v(2, lev, 2 * t_dev, LANES),
        v(2, lev, 2 * t_dev, LANES), v(2, lev, 2 * t_dev, LANES),
        v(2, t_dev, *tile), v(2, t_dev, *tile), v(2, t_dev, *tile), v(t_dev, *tile), v(5, 4, t_dev, *tile),
        v(2 * lev, LANES), v(2 * lev, LANES), v(2 * lev, LANES), v(2 * lev, LANES), v(2 * t_dev // 8, *tile),
        v(lev, *tile), v(lev, *tile), v(lev, *tile), v(lev, *tile), v(lev, *tile),
        v(lev, 24, LANES), v(lev, 24, LANES), v(24, LANES), v(6, *tile),
        dma((7 + nt,)), dma((6,)), dma((6,)),
        dma((nt,)), dma((nt,)), dma((nt,)), dma((nt,)),
        dma((nt,)), dma((nt,)), dma((nt,)), dma((nt,)), dma((nt,)), dma((nt,)),
        dma((2, 2, nt)), dma((2, 2, nt)), dma((2, 2)), dma((2, 2)), dma((2,)), dma((2,)),
    ]
    moved, grazed, factor = pl.pallas_call(
        functools.partial(kernel, (nt, nx, ny, t_dev, lev, t_dev * nt)),
        out_shape=(
            jax.ShapeDtypeStruct(tracers.shape, F32),
            jax.ShapeDtypeStruct(tracers.shape, F32),
            jax.ShapeDtypeStruct((nt, own, *tile), F32),
        ),
        in_specs=[pl.BlockSpec(memory_space=pltpu.HBM)] * 8,
        out_specs=[pl.BlockSpec(memory_space=pltpu.VMEM)] * 3,
        scratch_shapes=scratch,
        compiler_params=pltpu.CompilerParams(
            collective_id=0, has_side_effects=True, vmem_limit_bytes=20 * 1024 * 1024
        ),
        name="plankton",
    )(*[
        pltpu.with_memory_space_constraint(a, pltpu.HBM)
        for a in (tracers, fluxes, diff_east, diff_north, column_depth, grazers, groups, preference)
    ])
    return moved - factor.reshape(lev, *tile)[None] * grazed


def solution(mesh):
    placed = (
        P("tracer", None, "gx", "gy"),
        P(None, "tracer", "gx", "gy"),
        P("gx", "gy"),
        P("gx", "gy"),
        P("gx", "gy"),
        P(None, "gx", "gy"),
        P("tracer"),
        P(),
    )
    return jax.shard_map(
        on_device,
        mesh=mesh,
        in_specs=placed,
        out_specs=P("tracer", None, "gx", "gy"),
        check_vma=False,
    )
```

```python
import functools

import jax
import jax.numpy as jnp
from jax import lax
from jax.experimental import pallas as pl
from jax.experimental.pallas import tpu as pltpu
from jax.sharding import PartitionSpec as P

STEPS = 2
MESH = pl.DeviceIdType.MESH
F32 = jnp.float32
LANES = 128
LO, IN, HI = 6, 8, 16


def minmod(a, b):
    return jnp.maximum(0.0, jnp.minimum(a, b)) + jnp.minimum(0.0, jnp.maximum(a, b))


def roll(v, shift):
    return pltpu.roll(v, shift % LANES, 1)


def kernel(
    dims, tr, fl, de, dn, dep, gz, grp, prf, adv, grazed, f2,
    ext, dev, dnv, depv, gzv, grps, prfs, tv,
    cxs, cxl, cxh, cys, cyl, cyh, fa, fxs, fxl, fes, fel, fx,
    pqs, pqr, rs, rr, f1, own1,
    sxl, sxh, xl, xh, yp, yl, yr, ge, yst, gsl, gsh, gxl, gxh, tx,
    hy, fy, ky, hz, fz, hx, kx, wx, ec,
    lsem, csem, crec, fas, far, pqss, pqrs, rss, rrs, f1s, f1r, f2s, f2r,
    xss, xrs, yss, yrs, gss, grs,
):
    nt, nx, ny, t_dev, lev, total = dims
    own = lev // nt
    me, gx, gy = lax.axis_index("tracer"), lax.axis_index("gx"), lax.axis_index("gy")
    left, right = gy - 1, gy + 1
    has_left, has_right = gy > 0, gy < ny - 1
    has_lo, has_hi = gx > 0, gx < nx - 1
    others = [lax.rem(me + d, nt) for d in range(1, nt)]

    loads = [(fl, fa.at[me]), (de, dev), (dn, dnv), (dep, depv), (grp, grps), (prf, prfs), (gz, gzv)]
    for j in range(nt):
        c = pl.ds(j * own, own)
        loads.append((tr.at[:, c], ext.at[0, :, c, pl.ds(IN, 8), :]))
    loads = [pltpu.make_async_copy(a, b, lsem.at[i]) for i, (a, b) in enumerate(loads)]

    barrier = pltpu.get_barrier_semaphore()
    for peer in others:
        pl.semaphore_signal(barrier, inc=1, device_id={"tracer": peer}, device_id_type=MESH)

    @pl.when(has_left)
    def _():
        pl.semaphore_signal(barrier, inc=1, device_id={"gy": left}, device_id_type=MESH)

    @pl.when(has_right)
    def _():
        pl.semaphore_signal(barrier, inc=1, device_id={"gy": right}, device_id_type=MESH)

    @pl.when(has_lo)
    def _():
        pl.semaphore_signal(barrier, inc=1, device_id={"gx": gx - 1}, device_id_type=MESH)

    @pl.when(has_hi)
    def _():
        pl.semaphore_signal(barrier, inc=1, device_id={"gx": gx + 1}, device_id_type=MESH)

    for c in loads:
        c.start()

    lane = lax.broadcasted_iota(jnp.int32, (8, LANES), 1)
    row = lax.broadcasted_iota(jnp.int32, (8, LANES), 0)
    plev, e = lane // 8, lane % 8
    at_edge = (lane < 2) | (lane >= LANES - 2)
    zero = jnp.zeros((8, LANES), F32)

    def spread(v):
        base = jnp.where(lane < 8, roll(v, 4), zero)
        for s in (8, 16, 32, 64):
            base = base + roll(base, s)
        return base

    def send(src, dst, ssem, rsem, to):
        return pltpu.make_async_remote_copy(
            src_ref=src, dst_ref=dst, send_sem=ssem, recv_sem=rsem, device_id=to, device_id_type=MESH
        )

    fa_out = [
        send(fl, fa.at[me], fas.at[d], far.at[me], {"tracer": peer}) for d, peer in enumerate(others)
    ]

    near = [has_lo, has_hi, has_left, has_right]
    pl.semaphore_wait(barrier, nt - 1 + sum(h.astype(jnp.int32) for h in near))
    for c in fa_out:
        c.start()

    for c in loads[:6]:
        c.wait()
    for t in range(t_dev):
        w = jnp.full((8, LANES), prfs[grps[t]], F32)
        tv[t] = w
        tx[t // 4] = w if t % 4 == 0 else jnp.where(row // 2 == t % 4, w, tx[t // 4])
    depth = depv[...].astype(F32)
    cxs[0] = depth
    cxs[1] = dev[...]
    c_right = send(cys, cyl, csem.at[0], crec.at[0], {"gy": right})
    c_left = send(cys.at[pl.ds(0, 1)], cyh, csem.at[1], crec.at[1], {"gy": left})
    c_up = send(cxs, cxl, csem.at[2], crec.at[2], {"gx": gx + 1})
    c_down = send(cxs.at[pl.ds(0, 1)], cxh, csem.at[3], crec.at[3], {"gx": gx - 1})
    pl.when(has_hi)(c_up.start)
    pl.when(has_lo)(c_down.start)

    def y_copies(s):
        return (
            send(yp.at[s], yl.at[s], yss.at[s, 0], yrs.at[s, 0], {"gy": right}),
            send(yp.at[s], yr.at[s], yss.at[s, 1], yrs.at[s, 1], {"gy": left}),
        )

    def y_start(s):
        to_right, to_left = y_copies(s)
        pl.when(has_right)(to_right.start)
        pl.when(has_left)(to_left.start)

    def x_copies(s, j):
        c = pl.ds(j * own, own)
        return (
            send(sxh.at[s, c], xl.at[s, c], xss.at[s, 0, j], xrs.at[s, 0, j], {"gx": gx + 1}),
            send(sxl.at[s, c], xh.at[s, c], xss.at[s, 1, j], xrs.at[s, 1, j], {"gx": gx - 1}),
        )

    def gather_start(buf, ssem, rsem):
        for d, peer in enumerate(others):
            send(buf.at[me], buf.at[me], ssem.at[d], rsem.at[me], {"tracer": peer}).start()

    def gather_wait(buf, ssem, rsem):
        for d, peer in enumerate(others):
            send(buf.at[me], buf.at[peer], ssem.at[d], rsem.at[peer], {"tracer": peer}).wait_recv()

    def gather_done(buf, ssem, rsem):
        for d, peer in enumerate(others):
            send(buf.at[me], buf.at[peer], ssem.at[d], rsem.at[peer], {"tracer": peer}).wait_send()

    def scatter(src, dst, ssem, rsem, peer):
        return send(src.at[peer], dst.at[me], ssem.at[peer], rsem.at[me], {"tracer": peer})

    def scatter_wait(src, dst, ssem, rsem):
        for peer in others:
            send(src.at[peer], dst.at[peer], ssem.at[peer], rsem.at[peer], {"tracer": peer}).wait_recv()

    def x_start(s, j):
        up, down = x_copies(s, j)
        pl.when(has_hi)(up.start)
        pl.when(has_lo)(down.start)

    for j in range(nt):
        loads[7 + j].wait()
        for b in range(own):
            l = j * own + b
            p_sum, q_sum = zero, zero
            for t in range(t_dev):
                two, tile = pl.ds(2 * t, 2), ext[0, t, l, pl.ds(IN, 8), :]
                sxl[0, l, two, :] = ext[0, t, l, pl.ds(IN, 2), :]
                sxh[0, l, two, :] = ext[0, t, l, pl.ds(IN + 6, 2), :]
                w = tv[t]
                wc = w * tile
                p_sum = p_sum + wc
                q_sum = q_sum + w * wc
            pqs[j, b] = p_sum
            pqs[j, own + b] = q_sum
        x_start(0, j)

        @pl.when(j != me)
        def _():
            scatter(pqs, pqr, pqss, pqrs, j).start()


    cys[0] = spread(depth)
    cys[1] = spread(dnv[...])
    pl.when(has_right)(c_right.start)
    pl.when(has_left)(c_left.start)

    def pack_level(s, l, acc):
        tiles = [ext[s, t, l, pl.ds(IN, 8), :] for t in range(t_dev)]
        return tuple(
            jnp.where(plev == l, pltpu.roll(tiles[t], 8 * l + 4, 1), acc[t]) for t in range(t_dev)
        )

    blank = tuple(zero for _ in range(t_dev))
    acc = lax.fori_loop(0, lev, lambda l, acc: pack_level(0, l, acc), blank, unroll=4)
    for t in range(t_dev):
        yp[0, t] = acc[t]
    y_start(0)

    dn_low = 2.0 * roll(dnv[...], 1)
    depth_y = jnp.minimum(depth, roll(depth, 1))
    for l in range(lev):
        open_y = (depth_y > l).astype(F32)
        hy[l] = 0.5 * open_y
        ky[l] = dn_low * open_y
        if l:
            hz[l] = 0.5 * (depth > l).astype(F32)

    pl.when(has_left)(c_right.wait_recv)
    pl.when(has_right)(c_left.wait_recv)
    pl.when(has_hi)(c_down.wait_recv)

    @pl.when(has_lo)
    def _():
        c_up.wait_recv()

    @pl.when(gx == 0)
    def _():
        for k in range(2):
            cxl[k] = zero

    @pl.when(gx == nx - 1)
    def _():
        cxh[0] = zero

    @pl.when(gy == 0)
    def _():
        for k in range(2):
            cyl[k] = zero
        fel[...] = zero
        yl[...] = jnp.zeros_like(yl)

    @pl.when(gy == ny - 1)
    def _():
        cyh[0] = zero
        yr[...] = jnp.zeros_like(yr)

    dep_l, dep_r = cyl[0], cyh[0]
    dep_m = cys[0]
    plevf = plev.astype(F32)
    wet0 = (plevf < jnp.where(e < 4, dep_l, dep_m)).astype(F32)
    wet1 = (plevf < jnp.where(e < 4, dep_m, dep_r)).astype(F32)
    open0 = wet0 * roll(wet0, 1)
    open1 = wet1 * roll(wet1, 1)
    wx[...] = jnp.zeros_like(wx)
    wx[pl.ds(LO, 2), :] = cxl[0, pl.ds(6, 2), :]
    wx[pl.ds(IN, 8), :] = depth
    wx[pl.ds(HI, 2), :] = cxh[0, pl.ds(0, 2), :]
    d_low = jnp.concatenate([2.0 * cxl[1, pl.ds(7, 1), :], 2.0 * dev[pl.ds(0, 7), :]], axis=0)
    d_up = 2.0 * dev[...]
    depth_x = [
        jnp.minimum(wx[pl.ds(LO + k, 8), :], wx[pl.ds(LO + 1 + k, 8), :]) for k in range(4)
    ]
    for l in range(lev):
        opens = [(depth_x[k] > l).astype(F32) for k in range(4)]
        hx[l, pl.ds(IN - 1, 8), :] = 0.5 * opens[0]
        hx[l, pl.ds(IN + 2, 8), :] = 0.5 * opens[3]
        kx[l, pl.ds(IN, 8), :] = d_low * opens[1]
        kx[l, pl.ds(IN + 1, 8), :] = d_up * opens[2]
    for peer in others:
        send(fl, fa.at[peer], fas.at[0], far.at[peer], {"tracer": peer}).wait_recv()
    flux_edge = zero
    for l in range(lev):
        j, b = l // own, l % own
        flux_edge = jnp.where(plev == l, roll(fa[j, 1, b], 8 * l + 4), flux_edge)
        fxs[pl.ds(l, 1), :] = fa[j, 0, b, pl.ds(7, 1), :]
    fes[...] = flux_edge
    f_right = send(fes, fel, csem.at[4], crec.at[4], {"gy": right})
    f_up = send(fxs, fxl, csem.at[5], crec.at[5], {"gx": gx + 1})
    pl.when(has_right)(f_right.start)
    pl.when(has_hi)(f_up.start)

    loads[6].wait()
    for k in range(2 * own):
        pqr[me, k] = pqs[me, k]
    scatter_wait(pqs, pqr, pqss, pqrs)
    scale = 4.0 / total
    for b in range(own):
        prey = pqr[0, b]
        sq = pqr[0, own + b]
        for j in range(1, nt):
            prey = prey + pqr[j, b]
            sq = sq + pqr[j, own + b]
        f1[me, b] = gzv[me * own + b] / (1.0 + scale * prey)
        own1[b] = sq
    gather_start(f1, f1s, f1r)

    ec[0] = 0.5 * open0
    ec[1] = flux_edge
    ec[2] = 2.0 * open0 * roll(jnp.where(e < 4, cyl[1], cys[1]), 1)
    ec[3] = 0.5 * open1
    ec[4] = roll(flux_edge, 1) * open1
    ec[5] = 2.0 * open1 * roll(cys[1], 1)
    for l in range(lev):
        j, b = l // own, l % own
        fy[l] = roll(fa[j, 1, b], 1) * (depth_y > l).astype(F32)
        if l:
            fz[l] = fa[(l - 1) // own, 2, (l - 1) % own] * (depth > l).astype(F32)
        fx[l, pl.ds(IN, 8), :] = fa[j, 0, b]

    def edge(cells, h, flux, kappa):
        below = roll(cells, 1)
        jump = h * (cells - below)
        slope = minmod(jump, roll(jump, -1))
        carried = flux * jnp.where(flux > 0.0, below + roll(slope, 1), cells - slope) - kappa * jump
        return carried - roll(carried, -1)

    def y_edges(s):
        from_left, from_right = y_copies(s)
        pl.when(has_left)(from_left.wait_recv)
        pl.when(has_right)(from_right.wait_recv)
        for t in range(t_dev):
            mine = yp[s, t]
            low = edge(jnp.where(e < 4, yl[s, t], mine), ec[0], ec[1], ec[2])
            high = edge(jnp.where(e < 4, mine, yr[s, t]), ec[3], ec[4], ec[5])
            ge[t] = jnp.where(e < 4, high, low)

    def z_part(s):
        def pair(p, carry):
            for h in range(2):
                t = 2 * p + h
                cells = [ext[s, t, l, pl.ds(IN, 8), :] for l in range(lev)]
                jumps = [zero] + [hz[l] * (cells[l] - cells[l - 1]) for l in range(1, lev)] + [zero]
                slopes = [minmod(jumps[l], jumps[l + 1]) for l in range(lev)]
                faces = [zero]
                for l in range(1, lev):
                    f = fz[l]
                    faces.append(f * jnp.where(f > 0.0, cells[l - 1] + slopes[l - 1], cells[l] - slopes[l]))
                faces.append(zero)
                for l in range(lev):
                    adv[t, l] = cells[l] + (faces[l] - faces[l + 1])
            return carry

        lax.fori_loop(0, t_dev // 2, pair, 0)

    group = 4
    steps = lev // group

    def y_part(s):
        def jumps(g):
            for i in range(group):
                h = hy[g * group + i]
                for t in range(t_dev):
                    c = ext[s, t, g * group + i, pl.ds(IN, 8), :]
                    yst[0, i, t] = h * (c - roll(c, 1))

        def slopes(g):
            for i in range(group):
                for t in range(t_dev):
                    c, jump = ext[s, t, g * group + i, pl.ds(IN, 8), :], yst[0, i, t]
                    slope = minmod(jump, roll(jump, -1))
                    yst[1, i, t] = c + slope
                    yst[2, i, t] = c - slope
                    yst[3, i, t] = jump

        def fluxes(g):
            for i in range(group):
                f, k = fy[g * group + i], ky[g * group + i]
                ahead = f > 0.0
                for t in range(t_dev):
                    face = jnp.where(ahead, roll(yst[1, i, t], 1), yst[2, i, t])
                    yst[4, i, t] = f * face - k * yst[3, i, t]

        def tendencies(g):
            for i in range(group):
                l = g * group + i
                for t in range(t_dev):
                    carried = yst[4, i, t]
                    outer = zero if s else pltpu.roll(ge[t], (LANES - 4) - 8 * l, 1)
                    adv[t, l] = adv[t, l] + jnp.where(at_edge, outer, carried - roll(carried, -1))

        stages = (tendencies, fluxes, slopes, jumps)

        def step(g, carry):
            for k in range(4):
                stages[k](g - 3 + k)
            return carry

        for g in range(3):
            for m in range(g, -1, -1):
                stages[3 - m](g - m)
        lax.fori_loop(3, steps, step, 0)
        for g in range(steps, steps + 3):
            for m in range(3, g - steps, -1):
                stages[3 - m](g - m)

    def y_outer(l, carry):
        for t in range(t_dev):
            outer = pltpu.roll(ge[t], (LANES - 4) - 8 * l, 1)
            adv[t, l] = adv[t, l] + jnp.where(at_edge, outer, zero)
        return carry

    def x_part(s):
        def chunk(j, carry):
            up, down = x_copies(s, j)
            pl.when(has_lo)(up.wait_recv)
            pl.when(has_hi)(down.wait_recv)
            for b in range(own):
                l = j * own + b
                if s:
                    for halo, fac in ((xl, gxl), (xh, gxh)):
                        two = pl.multiple_of(2 * l, 2)
                        f8 = jnp.where(row % 2 == 0, fac[pl.ds(two, 1), :], fac[pl.ds(two + 1, 1), :])
                        for k in range(2 * t_dev // 8):
                            r = pl.ds(8 * k, 8)
                            halo[1, l, r, :] = halo[1, l, r, :] - (tx[k] * f8) * halo[0, l, r, :]
                h = [hx[l, pl.ds(IN - 1 + k, 8), :] for k in range(4)]
                f = [fx[l, pl.ds(IN - 1 + k, 8), :] for k in range(2)]
                kk = [kx[l, pl.ds(IN + k, 8), :] for k in range(2)]
                ahead = [f[k] > 0.0 for k in range(2)]
                total_r = zero
                for t in range(t_dev):
                    two = pl.ds(2 * t, 2)
                    ext[s, t, l, pl.ds(LO, 2), :] = xl[s, l, two, :]
                    ext[s, t, l, pl.ds(HI, 2), :] = xh[s, l, two, :]
                    c = [ext[s, t, l, pl.ds(LO + k, 8), :] for k in range(5)]
                    jump = [h[k] * (c[k + 1] - c[k]) for k in range(4)]
                    slope = [minmod(jump[k], jump[k + 1]) for k in range(3)]
                    carried = [
                        f[k] * jnp.where(ahead[k], c[k + 1] + slope[k], c[k + 2] - slope[k + 1])
                        - kk[k] * jump[k + 1]
                        for k in range(2)
                    ]
                    a = adv[t, l] + (carried[0] - carried[1])
                    adv[t, l] = a
                    if s == 0:
                        total_r = total_r + tv[t] * a
                        sxl[1, l, two, :] = adv[t, l, pl.ds(0, 2), :]
                        sxh[1, l, two, :] = adv[t, l, pl.ds(6, 2), :]
                if s == 0:
                    rs[j, b] = total_r
            if s == 0:
                @pl.when(j != me)
                def _():
                    scatter(rs, rr, rss, rrs, j).start()

                x_start(1, j)
            return carry

        lax.fori_loop(0, nt, chunk, 0)

    for s in range(STEPS):
        @pl.when(gx == 0)
        def _():
            xl[s] = jnp.zeros_like(xl[s])

        @pl.when(gx == nx - 1)
        def _():
            xh[s] = jnp.zeros_like(xh[s])

    z_part(0)
    pl.when(has_left)(f_right.wait_recv)
    ec[1] = roll(jnp.where(e < 4, fel[...], ec[1]), 1) * open0
    y_edges(0)
    y_part(0)
    pl.when(has_lo)(f_up.wait_recv)

    @pl.when(gx == 0)
    def _():
        fxl[...] = jnp.zeros_like(fxl)

    for l in range(lev):
        fx[l, pl.ds(IN - 1, 1), :] = fxl[pl.ds(l, 1), :]
    for l in range(lev):
        low = fx[l, pl.ds(IN - 1, 8), :] * (depth_x[1] > l).astype(F32)
        up = fx[l, pl.ds(IN, 8), :] * (depth_x[2] > l).astype(F32)
        fx[l, pl.ds(IN - 1, 8), :] = low
        fx[l, pl.ds(IN, 8), :] = up

    x_part(0)
    gather_wait(f1, f1s, f1r)
    for l in range(lev):
        gsl[pl.ds(2 * l, 2), :] = f1[l // own, l % own, pl.ds(0, 2), :]
        gsh[pl.ds(2 * l, 2), :] = f1[l // own, l % own, pl.ds(6, 2), :]
    g_up = send(gsh, gxl, gss.at[0], grs.at[0], {"gx": gx + 1})
    g_down = send(gsl, gxh, gss.at[1], grs.at[1], {"gx": gx - 1})
    pl.when(has_hi)(g_up.start)
    pl.when(has_lo)(g_down.start)

    def second(l, acc):
        acc = list(acc)
        j, b = l // own, lax.rem(l, own)
        factor = f1[j, b]
        for t in range(t_dev):
            c = adv[t, l] - (tv[t] * factor) * ext[0, t, l, pl.ds(IN, 8), :]
            ext[1, t, l, pl.ds(IN, 8), :] = c
            grazed[t, l] = tv[t] * c
            acc[t] = jnp.where(plev == l, pltpu.roll(c, 8 * l + 4, 1), acc[t])
        return tuple(acc)

    acc = lax.fori_loop(0, lev, second, blank, unroll=8)
    for t in range(t_dev):
        yp[1, t] = acc[t]
    y_start(1)
    z_part(1)
    y_part(1)

    for b in range(own):
        rr[me, b] = rs[me, b]
    scatter_wait(rs, rr, rss, rrs)
    for b in range(own):
        prey = rr[0, b]
        for j in range(1, nt):
            prey = prey + rr[j, b]
        prey = prey - f1[me, b] * own1[b]
        f2[me, b] = gzv[me * own + b] / (1.0 + scale * prey)
    gather_start(f2, f2s, f2r)

    pl.when(has_lo)(g_up.wait_recv)
    pl.when(has_hi)(g_down.wait_recv)

    @pl.when(gx == 0)
    def _():
        gxl[...] = jnp.zeros_like(gxl)

    @pl.when(gx == nx - 1)
    def _():
        gxh[...] = jnp.zeros_like(gxh)

    x_part(1)
    y_edges(1)
    lax.fori_loop(0, lev, y_outer, 0, unroll=8)
    gather_wait(f2, f2s, f2r)

    pl.when(has_right)(c_right.wait_send)
    pl.when(has_left)(c_left.wait_send)
    pl.when(has_hi)(c_up.wait_send)
    pl.when(has_lo)(c_down.wait_send)
    pl.when(has_hi)(g_up.wait_send)
    pl.when(has_lo)(g_down.wait_send)
    for s in range(STEPS):
        to_right, to_left = y_copies(s)
        pl.when(has_right)(to_right.wait_send)
        pl.when(has_left)(to_left.wait_send)
        for j in range(nt):
            up, down = x_copies(s, j)
            pl.when(has_hi)(up.wait_send)
            pl.when(has_lo)(down.wait_send)
    for c in fa_out:
        c.wait_send()
    pl.when(has_right)(f_right.wait_send)
    pl.when(has_hi)(f_up.wait_send)
    gather_done(f1, f1s, f1r)
    gather_done(f2, f2s, f2r)
    for peer in others:
        scatter(pqs, pqr, pqss, pqrs, peer).wait_send()
        scatter(rs, rr, rss, rrs, peer).wait_send()


def on_device(tracers, fluxes, diff_east, diff_north, column_depth, grazers, groups, preference):
    t_dev, lev, rows, cols = tracers.shape
    nt, nx, ny = (lax.axis_size(a) for a in ("tracer", "gx", "gy"))
    own = lev // nt
    tile = (8, LANES)
    dma = pltpu.SemaphoreType.DMA

    def v(*shape):
        return pltpu.VMEM(shape, F32)

    scratch = [
        v(2, t_dev, lev, 24, LANES),
        v(*tile), v(*tile), pltpu.VMEM(tile, jnp.int32), v(lev, *tile),
        pltpu.SMEM(groups.shape, jnp.int32), pltpu.SMEM(preference.shape, F32), v(t_dev, *tile),
        v(2, *tile), v(2, *tile), v(1, *tile), v(2, *tile), v(2, *tile), v(1, *tile),
        v(nt, 3, own, *tile), v(lev, LANES), v(lev, LANES), v(*tile), v(*tile), v(lev, 24, LANES),
        v(nt, 2 * own, *tile), v(nt, 2 * own, *tile), v(nt, own, *tile), v(nt, own, *tile),
        v(nt, own, *tile), v(own, *tile),
        v(2, lev, 2 * t_dev, LANES), v(2, lev, 2 * t_dev, LANES),
        v(2, lev, 2 * t_dev, LANES), v(2, lev, 2 * t_dev, LANES),
        v(2, t_dev, *tile), v(2, t_dev, *tile), v(2, t_dev, *tile), v(t_dev, *tile), v(5, 4, t_dev, *tile),
        v(2 * lev, LANES), v(2 * lev, LANES), v(2 * lev, LANES), v(2 * lev, LANES), v(2 * t_dev // 8, *tile),
        v(lev, *tile), v(lev, *tile), v(lev, *tile), v(lev, *tile), v(lev, *tile),
        v(lev, 24, LANES), v(lev, 24, LANES), v(24, LANES), v(6, *tile),
        dma((7 + nt,)), dma((6,)), dma((6,)),
        dma((nt,)), dma((nt,)), dma((nt,)), dma((nt,)),
        dma((nt,)), dma((nt,)), dma((nt,)), dma((nt,)), dma((nt,)), dma((nt,)),
        dma((2, 2, nt)), dma((2, 2, nt)), dma((2, 2)), dma((2, 2)), dma((2,)), dma((2,)),
    ]
    moved, grazed, factor = pl.pallas_call(
        functools.partial(kernel, (nt, nx, ny, t_dev, lev, t_dev * nt)),
        out_shape=(
            jax.ShapeDtypeStruct(tracers.shape, F32),
            jax.ShapeDtypeStruct(tracers.shape, F32),
            jax.ShapeDtypeStruct((nt, own, *tile), F32),
        ),
        in_specs=[pl.BlockSpec(memory_space=pltpu.HBM)] * 8,
        out_specs=[pl.BlockSpec(memory_space=pltpu.VMEM)] * 3,
        scratch_shapes=scratch,
        compiler_params=pltpu.CompilerParams(
            collective_id=0, has_side_effects=True, vmem_limit_bytes=20 * 1024 * 1024
        ),
        name="plankton",
    )(*[
        pltpu.with_memory_space_constraint(a, pltpu.HBM)
        for a in (tracers, fluxes, diff_east, diff_north, column_depth, grazers, groups, preference)
    ])
    return moved - factor.reshape(lev, *tile)[None] * grazed


def solution(mesh):
    placed = (
        P("tracer", None, "gx", "gy"),
        P(None, "tracer", "gx", "gy"),
        P("gx", "gy"),
        P("gx", "gy"),
        P("gx", "gy"),
        P(None, "gx", "gy"),
        P("tracer"),
        P(),
    )
    return jax.shard_map(
        on_device,
        mesh=mesh,
        in_specs=placed,
        out_specs=P("tracer", None, "gx", "gy"),
        check_vma=False,
    )
```
